32 devices in a mesh: req: 4 (over y, x), mlp: 8 (over z, core).
Axes of the slice: x: 2, y: 2, z: 4, core: 2. Of those that a mesh axis runs over, the one named last changes fastest.
Arguments:
- tokens: bfloat16 [64, 4608], P(('req', 'mlp')), may hold values from -6 to 6
- segments: int32 [4, 16], replicated, may hold values from 0 to 3, never falling along the last dimension, each value on 1 to 8 neighbouring positions
- owners: int32 [4], replicated, may hold values from 0 to 3, each once
- sink_keys: bfloat16 [4, 2048], P(None, 'mlp'), may hold values from -21 to 21
- sink_values: bfloat16 [4, 2048], P(None, 'mlp'), may hold values from -6 to 6
- window_keys: bfloat16 [4096, 2048], P('req', 'mlp'), may hold values from -6 to 6
- window_values: bfloat16 [4096, 2048], P('req', 'mlp'), may hold values from -6 to 6
- attn_gain: float32 [4608], replicated, may hold values from 0.1 to 1.9
- post_attn_gain: float32 [4608], replicated, may hold values from 0.1 to 1.9
- ffn_gain: float32 [4608], replicated, may hold values from 0.1 to 1.9
- post_ffn_gain: float32 [4608], replicated, may hold values from 0.1 to 1.9
- w_query: bfloat16 [4608, 4096], P(None, 'mlp'), may hold values from -0.09375 to 0.09375
- w_key: bfloat16 [4608, 2048], P(None, 'mlp'), may hold values from -0.25 to 0.25
- w_value: bfloat16 [4608, 2048], P(None, 'mlp'), may hold values from -0.09375 to 0.09375
- w_out: bfloat16 [4096, 4608], P('mlp'), may hold values from -0.09375 to 0.09375
- w_gate: bfloat16 [36864, 4608], P(('req', 'mlp')), may hold values from -0.09375 to 0.09375
- w_up: bfloat16 [36864, 4608], P(('req', 'mlp')), may hold values from -0.09375 to 0.09375
- w_down: bfloat16 [36864, 4608], P(('req', 'mlp')), may hold values from -0.03125 to 0.03125
Outputs:
- mixed: bfloat16 [64, 4608], P(('req', 'mlp'))
The draws below stay inside these ranges and needn't reach their ends.
Inputs may be any that keep to these rules, and one draw needn't show every extreme that they name: `segments`: row g gives, for the 16 suffix tokens of request group g in order, which of the group's 4 requests each belongs to; a request's tokens are contiguous and its number never falls along the row. Req index d holds array rows d * B to d * B + B - 1 of window_keys and window_values, whose window positions are owners[d] * B to owners[d] * B + B - 1, B = 4096 / 4; every block of positions is held once.
All inputs are finite; a program needn't handle non-finite values.
Results may differ from the reference program's by a relative error of at most 0.015.
Values may be sent and summed in bfloat16 or wider, within the bound.
A program may use at most 128 MiB of HBM per device.

```python
import math
import jax
import jax.numpy as jnp
import numpy as np
from jax import lax

D = 4608
HEADS = 32
KVH = 16
HD = 128
FF = 36864
WIN = 4096
SINK = 4
REQ_GRP = 4
GTOK = 16
TOKENS = 64
N_REQ = 4


def block_scale(stream_key, extent, cuts, low, largest):
    level, own = 1.0, jax.random.fold_in(stream_key, 6)
    for position, parts in cuts:
        draws = jnp.exp(jax.random.uniform(jax.random.fold_in(own, position), (parts,), jnp.float32, low / len(cuts), largest / len(cuts)))
        level = level * jnp.repeat(draws, extent[position] // parts).reshape([-1 if axis == position else 1 for axis in range(len(extent))])
    return level


def split_up(number_of, total, bound, slope):
    weights = [(1 << 20) // math.isqrt(standing ** slope) + 1 for standing in range(2, number_of + 1)]
    spare, holding = total - bound - (number_of - 1), [1] * (number_of - 1)
    while spare > 0:
        movable = [i for i in range(number_of - 1) if holding[i] < bound]
        whole, left = sum([weights[i] for i in movable]), spare
        for i in movable:
            extra = min(bound - holding[i], max(1, left * weights[i] // whole), spare)
            holding[i] = holding[i] + extra
            spare = spare - extra
    return np.array([bound] + holding)


def ragged_sizes(key, count, total, most, skew):
    if count == 2:
        one = jax.random.randint(key, (), max(1, total - most), min(most, total - 1) + 1)
        return jnp.stack([one, total - one])
    tallies = jnp.asarray(split_up(count, total, most, skew), jnp.int32)
    pairs = (count - 1) // 2
    source_of, sink = tallies[1:1 + 2 * pairs:2], tallies[2:2 + 2 * pairs:2]
    margin = jnp.minimum(source_of - 1, most - sink)
    shifted = jax.random.randint(jax.random.fold_in(key, 1), (pairs,), 0, 1 << 20) % (margin + 1)
    tallies = tallies.at[1:1 + 2 * pairs:2].set(source_of - shifted).at[2:2 + 2 * pairs:2].set(sink + shifted)
    return tallies[jax.random.permutation(jax.random.fold_in(key, 2), count)]


def centred(own_key, extent, width, reach, cuts=(), held_as=jnp.bfloat16):
    values = jax.random.normal(own_key, extent, jnp.float32) * width
    if len(cuts) > 0:
        values = block_scale(own_key, extent, cuts, -0.22, 0.18) * values
    return jnp.clip(values, min=-reach, max=reach).astype(held_as)


def setup_inputs(seed: int = 0) -> dict:
    seeds = jax.random.split(jax.random.key(seed), 19)
    tokens = centred(seeds[0], (TOKENS, D), 1.0, 6.0, ((0, 32),))
    segments = jax.vmap(lambda own: jnp.searchsorted(jnp.cumsum(ragged_sizes(own, REQ_GRP, GTOK, GTOK // 2, 2)), jnp.arange(GTOK), side="right"))(jax.random.split(seeds[1], N_REQ)).reshape((N_REQ, GTOK)).astype(jnp.int32)
    owners = jax.random.permutation(seeds[2], N_REQ).astype(jnp.int32)
    sink_keys = centred(seeds[3], (SINK, KVH * HD), 3.5, 21.0, ((1, 8),))
    sink_values = centred(seeds[4], (SINK, KVH * HD), 1.0, 6.0, ((1, 8),))
    window_keys = centred(seeds[5], (WIN, KVH * HD), 1.0, 6.0, ((0, 4), (1, 8)))
    window_values = centred(seeds[6], (WIN, KVH * HD), 1.0, 6.0, ((0, 4), (1, 8)))
    attn_gain = jnp.clip(1.0 + 0.18 * jax.random.normal(seeds[7], (D,), jnp.float32), 0.1, 1.9)
    post_attn_gain = jnp.clip(1.0 + 0.18 * jax.random.normal(seeds[8], (D,), jnp.float32), 0.1, 1.9)
    ffn_gain = jnp.clip(1.0 + 0.18 * jax.random.normal(seeds[9], (D,), jnp.float32), 0.1, 1.9)
    post_ffn_gain = jnp.clip(1.0 + 0.18 * jax.random.normal(seeds[10], (D,), jnp.float32), 0.1, 1.9)
    w_query = centred(seeds[11], (D, HEADS * HD), D ** -0.5, 0.09375, ((1, 8),))
    w_key = centred(seeds[12], (D, KVH * HD), (D // 9) ** -0.5, 0.25, ((1, 8),))
    w_value = centred(seeds[13], (D, KVH * HD), D ** -0.5, 0.09375, ((1, 8),))
    w_out = centred(seeds[14], (HEADS * HD, D), (HEADS * HD) ** -0.5, 0.09375, ((0, 8),))
    w_gate = centred(seeds[15], (FF, D), D ** -0.5, 0.09375, ((0, 32),))
    w_up = centred(seeds[16], (FF, D), D ** -0.5, 0.09375, ((0, 32),))
    w_down = centred(seeds[17], (FF, D), FF ** -0.5, 0.03125, ((0, 32),))
    return dict(tokens=tokens, segments=segments, owners=owners, sink_keys=sink_keys, sink_values=sink_values, window_keys=window_keys, window_values=window_values, attn_gain=attn_gain, post_attn_gain=post_attn_gain, ffn_gain=ffn_gain, post_ffn_gain=post_ffn_gain, w_query=w_query, w_key=w_key, w_value=w_value, w_out=w_out, w_gate=w_gate, w_up=w_up, w_down=w_down)


epsilon = 1e-06
soft_cap = 50.0
logit_scale = 1.0 / 12.0

def rms_scale(values):
    return values * lax.rsqrt(lax.optimization_barrier(jnp.mean(values * values, axis=-1, keepdims=True)) + epsilon)

def positions(seg_rows):
    ordering = jnp.arange(seg_rows.shape[-1], dtype=jnp.int32)
    same_seg = seg_rows[..., :, None] == seg_rows[..., None, :]
    earlier = ordering[None, :] < ordering[:, None]
    return lax.optimization_barrier(jnp.sum((same_seg & earlier).astype(jnp.int32), axis=-1)).astype(jnp.int32)

def attend(query_rows, key_matrix_rows, value_matrix_rows, visible):
    score_matrix = jnp.einsum('woji,roi->wojr', query_rows.astype(jnp.float32), key_matrix_rows.astype(jnp.float32)) * logit_scale
    weight = jnp.exp(soft_cap * jnp.tanh(score_matrix / soft_cap))
    weight = jnp.where(visible[:, None, None, :], weight, jnp.zeros_like(weight))
    totals = lax.optimization_barrier(jnp.sum(weight, axis=-1))
    rounded_output = lax.optimization_barrier(weight.astype(jnp.bfloat16)).astype(jnp.float32)
    summed_output = jnp.einsum('xfka,afq->xfkq', rounded_output, value_matrix_rows.astype(jnp.float32))
    return (summed_output, totals)

def reference(tokens, segments, owners, sink_keys, sink_values, window_keys, window_values, attn_gain, post_attn_gain, ffn_gain, post_ffn_gain, w_query, w_key, w_value, w_out, w_gate, w_up, w_down):
    per_kv = HEADS // KVH
    block_rows = WIN // N_REQ
    row_ids = jnp.arange(WIN, dtype=jnp.int32)
    window_pos = (owners[row_ids // block_rows] * block_rows + row_ids % block_rows).astype(jnp.int32)
    window_key = window_keys.reshape(WIN, KVH, HD)
    window_value = window_values.reshape(WIN, KVH, HD)
    sink_key = sink_keys.reshape(SINK, KVH, HD)
    sink_value = sink_values.reshape(SINK, KVH, HD)
    pos_all = positions(segments)
    token_float = tokens.astype(jnp.float32)
    normed = (rms_scale(token_float) * attn_gain).astype(jnp.bfloat16)
    ordering = jnp.arange(GTOK, dtype=jnp.int32)

    def one_group(group_index):
        group_rows = lax.dynamic_slice_in_dim(normed, (group_index * GTOK).astype(jnp.int32), GTOK, 0)
        query_rows = jnp.dot(group_rows, w_query, preferred_element_type=jnp.float32).astype(jnp.bfloat16).reshape(GTOK, KVH, per_kv, HD)
        key_new = jnp.dot(group_rows, w_key, preferred_element_type=jnp.float32).astype(jnp.bfloat16).reshape(GTOK, KVH, HD)
        value_new = jnp.dot(group_rows, w_value, preferred_element_type=jnp.float32).astype(jnp.bfloat16).reshape(GTOK, KVH, HD)
        seg_row = lax.dynamic_index_in_dim(segments, group_index, 0, keepdims=False)
        pos_row = lax.dynamic_index_in_dim(pos_all, group_index, 0, keepdims=False)
        sink_sum, sink_tot = attend(query_rows, sink_key, sink_value, jnp.ones((GTOK, SINK), dtype=jnp.bool_))
        win_sum, win_tot = attend(query_rows, window_key, window_value, window_pos[None, :] > pos_row[:, None])
        local_vis = (seg_row[:, None] == seg_row[None, :]) & (ordering[None, :] <= ordering[:, None])
        loc_sum, loc_tot = attend(query_rows, key_new, value_new, local_vis)
        merged = (sink_sum + win_sum + loc_sum) / (sink_tot + win_tot + loc_tot)[..., None]
        return merged.astype(jnp.bfloat16).reshape(GTOK, HEADS * HD)
    attended = lax.map(one_group, jnp.arange(N_REQ, dtype=jnp.int32)).reshape(TOKENS, HEADS * HD)
    projected = jnp.dot(attended, w_out, preferred_element_type=jnp.float32)
    residual = token_float + rms_scale(projected) * post_attn_gain
    ffn_in = (rms_scale(residual) * ffn_gain).astype(jnp.bfloat16)
    contract = (((1,), (1,)), ((), ()))
    gate_part = lax.dot_general(ffn_in, w_gate, contract, preferred_element_type=jnp.float32)
    up_part = lax.dot_general(ffn_in, w_up, contract, preferred_element_type=jnp.float32)
    hidden = (jax.nn.gelu(gate_part, approximate=True) * up_part).astype(jnp.bfloat16)
    ffn_out = jnp.dot(hidden, w_down, preferred_element_type=jnp.float32)
    return (residual + rms_scale(ffn_out) * post_ffn_gain).astype(jnp.bfloat16)
```

```python
import functools
import math

import jax
import jax.numpy as jnp
from jax import lax
from jax.experimental import pallas as pl
from jax.experimental.pallas import tpu as pltpu
from jax.sharding import PartitionSpec as P

HD = 128
EPS = 1e-06
SOFT_CAP = 50.0
SCORE_SCALE = 1.0 / (12.0 * SOFT_CAP)
MESH = pl.DeviceIdType.MESH
F32 = jnp.float32
BF16 = jnp.bfloat16
NT = (((1,), (1,)), ((), ()))
GELU_C = math.sqrt(2.0 / math.pi)


def rms_scale(values):
    return values * lax.rsqrt(jnp.mean(values * values, axis=-1, keepdims=True) + EPS)


def weights_of(scores):
    return jnp.exp(SOFT_CAP * jnp.tanh(scores * SCORE_SCALE))


def chunks(total, size):
    return [(start, min(size, total - start)) for start in range(0, total, size)]


def kernel(
    n_req, n_mlp,
    tok_hbm, seg_hbm, own_hbm, sk_hbm, sv_hbm, gains_a, gains_pa, gains_f, gains_pf,
    wk_hbm, wv_hbm, wq_hbm, wkey_hbm, wval_hbm, wo_hbm, wg_hbm, wu_hbm, wd_hbm,
    out,
    tok, segments, owners, sink_k, sink_v,
    win_k, win_v, wq, wkey, wval, wo, wg, wu, wd,
    attn_gain, post_attn_gain, ffn_gain, post_ffn_gain, load_sem,
    posv, segv,
    ag1, xr, qbuf, ekf, evf, psend, prec,
    pj, s1, r1, s3, r3, head_sum,
    ag2, xf, xb, hg, hu, hid, acc,
    t1, u1, t2, u2, t3f, t3, u3,
    ss_ag1z, rs_ag1z, ss_ag1c, rs_ag1c, ss_q, rs_q, ss_p, rs_p,
    ss_1, rs_1, ss_3, rs_3,
    ss_ag2z, rs_ag2z, ss_ag2r, rs_ag2r, ss_ag2c, rs_ag2c,
    ss_t1, rs_t1, ss_t2, rs_t2, ss_t3, rs_t3,
):
    n_z = n_mlp // 2
    rq = lax.axis_index("req")
    me = lax.axis_index("mlp")
    z = me // 2
    c = me % 2
    oc = 1 - c
    sib = z * 2 + oc
    tp, width = tok.shape
    group = tp * n_mlp
    span = n_z * tp
    total = group * n_req
    kv_cols = wkey.shape[1]
    q_cols = wq.shape[1]
    kv_heads = kv_cols // HD
    pieces, cols = ag2.shape[0], ag2.shape[-1]

    def z_other(step):
        index, weight = 0, 1
        while weight < n_z:
            bit = (z // weight) % 2
            index = index + weight * (1 - bit if step & weight else bit)
            weight *= 2
        return index

    def z_peer(step):
        return {"mlp": z_other(step) * 2 + c}

    def r_peer(step):
        return lax.rem(rq + step, n_req)

    z_far_first = list(range(n_z - 1, 0, -1))

    barrier = pltpu.get_barrier_semaphore()
    for step in z_far_first:
        pl.semaphore_signal(barrier, inc=1, device_id=z_peer(step), device_id_type=MESH)
    for step in range(1, n_req):
        pl.semaphore_signal(barrier, inc=1, device_id={"req": r_peer(step)}, device_id_type=MESH)
    pl.semaphore_signal(barrier, inc=1, device_id={"mlp": sib}, device_id_type=MESH)

    loads = {}
    for number, (name, src, dst) in enumerate((
        ("tok", tok_hbm, tok), ("ga", gains_a, attn_gain.at[0]),
        ("seg", seg_hbm, segments), ("own", own_hbm, owners),
        ("q", wq_hbm, wq), ("k", wkey_hbm, wkey), ("v", wval_hbm, wval),
        ("sk", sk_hbm, sink_k), ("sv", sv_hbm, sink_v),
        ("wk", wk_hbm, win_k), ("wv", wv_hbm, win_v), ("o", wo_hbm, wo),
        ("gpa", gains_pa, post_attn_gain.at[0]), ("gf", gains_f, ffn_gain.at[0]),
        ("gpf", gains_pf, post_ffn_gain.at[0]),
        ("g", wg_hbm, wg), ("u", wu_hbm, wu), ("d", wd_hbm, wd),
    )):
        loads[name] = pltpu.make_async_copy(src, dst, load_sem.at[number])
        loads[name].start()

    sent = []

    def send(src, dst, send_sem, recv_sem, device):
        copy = pltpu.make_async_remote_copy(
            src_ref=src, dst_ref=dst, send_sem=send_sem, recv_sem=recv_sem,
            device_id=device, device_id_type=MESH,
        )
        copy.start()
        sent.append(copy)
        return copy

    def settle():
        for copy in sent:
            copy.wait_send()
        sent.clear()

    loads["tok"].wait()
    loads["ga"].wait()
    token_float = tok[...].astype(F32)
    ag1[c, z] = (rms_scale(token_float) * attn_gain[...]).astype(BF16)
    pl.semaphore_wait(barrier, n_z + n_req - 1)
    z_copies = {
        k: send(ag1.at[c, z], ag1.at[c, z], ss_ag1z.at[k], rs_ag1z.at[k], z_peer(k))
        for k in z_far_first
    }
    c_copies = [send(ag1.at[c, z], ag1.at[c, z], ss_ag1c.at[0], rs_ag1c.at[0], {"mlp": sib})]

    def row_of_token(t):
        device, inner = t // tp, t % tp
        return (device % 2) * span + (device // 2) * tp + inner

    loads["seg"].wait()
    loads["own"].wait()
    for g in range(n_req):
        at = jnp.int32(0)
        for t in range(group):
            if t:
                at = jnp.where(segments[g, t] == segments[g, t - 1], at + 1, 0)
            row = g * group + row_of_token(t)
            posv[row:row + 1, :] = jnp.full((1, HD), at, jnp.int32)
    extra = 2 * group
    column = lax.broadcasted_iota(jnp.int32, (group, extra), 1)
    row_at = lax.broadcasted_iota(jnp.int32, (group, extra), 0)
    seg_row = jnp.full((group, extra), -1, jnp.int32)
    column_token = jnp.full((group, extra), group, jnp.int32)
    row_token = jnp.zeros((group, extra), jnp.int32)
    for t in range(group):
        row = row_of_token(t)
        segv[row:row + 1, :] = jnp.full((1, extra), segments[rq, t], jnp.int32)
        seg_row = jnp.where(column == row, segments[rq, t], seg_row)
        column_token = jnp.where(column == row, t, column_token)
        row_token = jnp.where(row_at == row, t, row_token)
    n_sink = sink_k.shape[0]
    local = (segv[...] == seg_row) & (column_token <= row_token)
    sinks = (column >= group) & (column < group + n_sink)
    one = jnp.where(local | sinks, 1, 0)
    emask = jnp.concatenate([one, one], axis=0) > 0
    block_rows = win_k.shape[0]
    wpos = owners[rq] * block_rows + lax.broadcasted_iota(jnp.int32, (1, block_rows), 1)

    for k in range(1, n_z):
        z_copies[k].wait_recv()
        block = ag1.at[c, z_other(k)]
        c_copies.append(send(block, block, ss_ag1c.at[k], rs_ag1c.at[k], {"mlp": sib}))
    for copy in c_copies:
        copy.wait_recv()
    for core in range(2):
        for level in range(n_z):
            row = core * span + level * tp
            xr[row:row + tp, :] = ag1[core, level].astype(F32)
    rows = xr[...].astype(BF16)

    loads["q"].wait()
    qbuf[rq] = jnp.dot(rows, wq[...], preferred_element_type=F32).astype(BF16)
    q_copies = [
        send(qbuf.at[rq], qbuf.at[rq], ss_q.at[k], rs_q.at[k], {"req": r_peer(k)})
        for k in range(1, n_req)
    ]
    loads["k"].wait()
    key_new = jnp.dot(rows, wkey[...], preferred_element_type=F32).astype(BF16)
    loads["v"].wait()
    value_new = jnp.dot(rows, wval[...], preferred_element_type=F32).astype(BF16)
    loads["sk"].wait()
    loads["sv"].wait()
    for target, new, sinks in ((ekf, key_new, sink_k), (evf, value_new, sink_v)):
        target[...] = jnp.zeros_like(target)
        target[0:group, :] = new.astype(F32)
        target[group:group + n_sink, :] = sinks[...].astype(F32)

    own_q = qbuf[rq]
    extra_k = ekf[...].astype(BF16)
    extra_v = evf[...].astype(BF16)
    own_num, own_den = [], []
    for j in range(kv_heads):
        lanes = slice(j * HD, (j + 1) * HD)
        pair = jnp.concatenate(
            [own_q[:, (2 * j + i) * HD:(2 * j + i + 1) * HD] for i in range(2)], axis=0)
        scores = lax.dot_general(pair, extra_k[:, lanes], NT, preferred_element_type=F32)
        weight = jnp.where(emask, weights_of(scores), 0.0)
        den = jnp.sum(weight, axis=-1, keepdims=True)
        num = jnp.dot(weight.astype(BF16), extra_v[:, lanes], preferred_element_type=F32)
        for i in range(2):
            own_num.append(num[i * group:(i + 1) * group])
            own_den.append(den[i * group:(i + 1) * group])

    visible = wpos > posv[:, 0:1]
    visible = jnp.where(visible, 1, 0)
    visible = jnp.concatenate([visible, visible], axis=0) > 0
    lane = lax.broadcasted_iota(jnp.int32, (total, HD), 1)
    loads["wk"].wait()
    loads["wv"].wait()
    for copy in q_copies:
        copy.wait_recv()
    all_q = qbuf[...].reshape(total, q_cols)
    p_copies = {}
    for j in range(kv_heads):
        lanes = slice(j * HD, (j + 1) * HD)
        pair = jnp.concatenate(
            [all_q[:, (2 * j + i) * HD:(2 * j + i + 1) * HD] for i in range(2)], axis=0)
        scores = lax.dot_general(pair, win_k[:, lanes], NT, preferred_element_type=F32)
        weight = jnp.where(visible, weights_of(scores), 0.0)
        den = jnp.sum(weight, axis=-1, keepdims=True)
        num = jnp.dot(weight.astype(BF16), win_v[:, lanes], preferred_element_type=F32)
        dens = jnp.zeros((total, HD), F32)
        for i in range(2):
            rows_i = slice(i * total, (i + 1) * total)
            psend[:, j, :, i * HD:(i + 1) * HD] = num[rows_i].astype(BF16).reshape(n_req, group, HD)
            high = den[rows_i].astype(BF16).astype(F32)
            dens = jnp.where(lane == 2 * i, high, dens)
            dens = jnp.where(lane == 2 * i + 1, den[rows_i] - high, dens)
        psend[:, j, :, 2 * HD:] = dens.astype(BF16).reshape(n_req, group, HD)
        for k in range(1, n_req):
            p_copies[j, k] = send(
                psend.at[r_peer(k), j], prec.at[k - 1, j], ss_p.at[j, k], rs_p.at[j, k],
                {"req": r_peer(k)})
    heads = []
    for j in range(kv_heads):
        partial = psend[rq, j].astype(F32)
        for k in range(1, n_req):
            p_copies[j, k].wait_recv()
            partial = partial + prec[k - 1, j].astype(F32)
        for i in range(2):
            num = own_num[2 * j + i] + partial[:, i * HD:(i + 1) * HD]
            base = 2 * HD + 2 * i
            den = own_den[2 * j + i] + partial[:, base:base + 1] + partial[:, base + 1:base + 2]
            heads.append((num / den).astype(BF16))
    attended = jnp.concatenate(heads, axis=1)

    def lanes_of(j):
        return slice(j * cols, (j + 1) * cols)

    loads["o"].wait()
    c_copies = []
    for j in range(pieces):
        pj[j] = jnp.dot(
            attended, wo[:, lanes_of(j)], preferred_element_type=F32).reshape(2, span, cols)
        s1[j] = pj[j, oc].astype(BF16)
        c_copies.append(send(s1.at[j], r1.at[j], ss_1.at[j], rs_1.at[j], {"mlp": sib}))
    z_copies = {}
    for j in range(pieces):
        c_copies[j].wait_recv()
        both = pj[j, c] + r1[j].astype(F32)
        for level in range(n_z):
            head_sum[j, level] = both[level * tp:(level + 1) * tp]
            s3[j, level] = both[level * tp:(level + 1) * tp].astype(BF16)
        for k in z_far_first:
            z_copies[j, k] = send(
                s3.at[j, z_other(k)], r3.at[j, k - 1], ss_3.at[j, k], rs_3.at[j, k], z_peer(k))
    for name in ("gpa", "gf", "gpf"):
        loads[name].wait()
    projected, residual = [], []
    squares = jnp.zeros((tp, 1), F32)
    for j in range(pieces):
        total_j = head_sum[j, z]
        for k in range(1, n_z):
            z_copies[j, k].wait_recv()
            total_j = total_j + r3[j, k - 1].astype(F32)
        projected.append(total_j)
        squares = squares + jnp.sum(total_j * total_j, axis=-1, keepdims=True)
    scale = lax.rsqrt(squares / width + EPS)
    squares = jnp.zeros((tp, 1), F32)
    for j in range(pieces):
        part = token_float[:, lanes_of(j)] + projected[j] * scale * post_attn_gain[:, lanes_of(j)]
        residual.append(part)
        squares = squares + jnp.sum(part * part, axis=-1, keepdims=True)
    scale = lax.rsqrt(squares / width + EPS)

    z_copies, r_copies, c_copies = {}, {}, {}

    def spread(j, step):
        level = z_other(step)
        for k in range(1, n_req):
            r_copies[j, step, k] = send(
                ag2.at[j, 0, 0, level], ag2.at[j, 0, k, level], ss_ag2r.at[j, step, k],
                rs_ag2r.at[j, step, k], {"req": r_peer(k)})

    def cross(j, k):
        c_copies[j, k] = send(
            ag2.at[j, 0, k], ag2.at[j, 1, k], ss_ag2c.at[j, k], rs_ag2c.at[j, k], {"mlp": sib})

    def unpack(j, core, k):
        base = (core * n_req + k) * span
        for level in range(n_z):
            xf[base + level * tp:base + (level + 1) * tp, :] = ag2[j, core, k, level].astype(F32)

    for j in range(pieces):
        ag2[j, 0, 0, z] = (residual[j] * scale * ffn_gain[:, lanes_of(j)]).astype(BF16)
        for k in range(1, n_z):
            z_copies[j, k] = send(
                ag2.at[j, 0, 0, z], ag2.at[j, 0, 0, z], ss_ag2z.at[j, k], rs_ag2z.at[j, k],
                z_peer(k))
        spread(j, 0)
    for j in range(pieces):
        for step in range(1, n_z):
            z_copies[j, step].wait_recv()
            spread(j, step)
        cross(j, 0)

    def collect(j):
        for k in range(1, n_req):
            for step in range(n_z):
                r_copies[j, step, k].wait_recv()
            cross(j, k)

    collect(0)
    for j in range(pieces):
        for k in range(n_req):
            unpack(j, 0, k)
        for k in range(n_req):
            c_copies[j, k].wait_recv()
            unpack(j, 1, k)
        xb[...] = xf[...].astype(BF16)
        if j == 0:
            loads["g"].wait()
        gate = lax.dot_general(xb[...], wg[:, lanes_of(j)], NT, preferred_element_type=F32)
        if j:
            gate = gate + hg[...]
        hg[...] = gate
        if j == 0:
            loads["u"].wait()
        if j + 1 < pieces:
            collect(j + 1)
        up = lax.dot_general(xb[...], wu[:, lanes_of(j)], NT, preferred_element_type=F32)
        if j:
            up = up + hu[...]
        hu[...] = up
    gate = hg[...]
    inner = GELU_C * (gate + 0.044715 * (gate * gate * gate))
    hid[...] = (0.5 * gate * (1.0 + jnp.tanh(inner)) * hu[...]).astype(BF16)
    loads["d"].wait()

    first, second, third, finals = {}, {}, {}, []
    half = n_req * span
    for j in range(pieces):
        sums = jnp.dot(hid[...], wd[:, lanes_of(j)], preferred_element_type=F32)
        t1[j] = sums[half:].astype(BF16)
        acc[j] = sums[:half]
        first[j] = send(t1.at[j], u1.at[j], ss_t1.at[j], rs_t1.at[j], {"mlp": sib})
    for j in range(pieces):
        first[j].wait_recv()
        both = acc[j] + u1[j].astype(F32)
        for k in range(n_req - 1, 0, -1):
            t2[j, k] = both[k * span:(k + 1) * span].astype(BF16)
            second[j, k] = send(
                t2.at[j, k], u2.at[j, k], ss_t2.at[j, k], rs_t2.at[j, k],
                {"req": r_peer(n_req - k)})
        acc[j, 0:span] = both[:span]
    for j in range(pieces):
        both = acc[j, 0:span]
        for k in range(1, n_req):
            second[j, k].wait_recv()
            both = both + u2[j, k].astype(F32)
        for level in range(n_z):
            t3f[j, level] = both[level * tp:(level + 1) * tp]
            t3[j, level] = both[level * tp:(level + 1) * tp].astype(BF16)
        for k in z_far_first:
            third[j, k] = send(
                t3.at[j, z_other(k)], u3.at[j, k], ss_t3.at[j, k], rs_t3.at[j, k], z_peer(k))
    settle()
    squares = jnp.zeros((tp, 1), F32)
    for j in range(pieces):
        total_j = t3f[j, z]
        for k in range(1, n_z):
            third[j, k].wait_recv()
            total_j = total_j + u3[j, k].astype(F32)
        finals.append(total_j)
        squares = squares + jnp.sum(total_j * total_j, axis=-1, keepdims=True)
    scale = lax.rsqrt(squares / width + EPS)
    for j in range(pieces):
        out[:, lanes_of(j)] = (
            residual[j] + finals[j] * scale * post_ffn_gain[:, lanes_of(j)]).astype(BF16)


def shards(
    n_req, n_mlp,
    tokens, segments, owners, sink_keys, sink_values, window_keys, window_values,
    attn_gain, post_attn_gain, ffn_gain, post_ffn_gain,
    w_query, w_key, w_value, w_out, w_gate, w_up, w_down,
):
    tp, width = tokens.shape
    n_z = n_mlp // 2
    group = tp * n_mlp
    span = n_z * tp
    total = group * n_req
    q_cols, kv_cols, ff = w_query.shape[1], w_key.shape[1], w_gate.shape[0]
    kv_heads = kv_cols // HD
    extra = 2 * group
    pieces = 3 if n_req <= 4 else 1
    cols = width // pieces

    def v(shape, dtype=BF16):
        return pltpu.VMEM(shape, dtype)

    dma = pltpu.SemaphoreType.DMA
    scratch = [
        v(tokens.shape), pltpu.SMEM(segments.shape, jnp.int32), pltpu.SMEM(owners.shape, jnp.int32),
        v(sink_keys.shape), v(sink_values.shape)]
    scratch += [v(a.shape) for a in (
        window_keys, window_values, w_query, w_key, w_value, w_out, w_gate, w_up, w_down)]
    scratch += [v((1, width), F32)] * 4
    scratch += [
        dma((18,)),
        v((total, HD), jnp.int32), v((group, extra), jnp.int32),
        v((2, n_z, tp, width)), v((group, width), F32),
        v((n_req, group, q_cols)), v((extra, kv_cols), F32), v((extra, kv_cols), F32),
        v((n_req, kv_heads, group, 3 * HD)), v((n_req - 1, kv_heads, group, 3 * HD)),
        v((pieces, 2, span, cols), F32), v((pieces, span, cols)), v((pieces, span, cols)),
        v((pieces, n_z, tp, cols)), v((pieces, n_z - 1, tp, cols)),
        v((pieces, n_z, tp, cols), F32),
        v((pieces, 2, n_req, n_z, tp, cols)), v((total, cols), F32), v((total, cols)),
        v((total, ff), F32), v((total, ff), F32), v((total, ff)),
        v((pieces, n_req * span, cols), F32),
        v((pieces, n_req * span, cols)), v((pieces, n_req * span, cols)),
        v((pieces, n_req, span, cols)), v((pieces, n_req, span, cols)),
        v((pieces, n_z, tp, cols), F32), v((pieces, n_z, tp, cols)), v((pieces, n_z, tp, cols)),
        dma((n_z,)), dma((n_z,)), dma((n_z,)), dma((n_z,)),
        dma((n_req,)), dma((n_req,)), dma((kv_heads, n_req)), dma((kv_heads, n_req)),
        dma((pieces,)), dma((pieces,)), dma((pieces, n_z)), dma((pieces, n_z)),
        dma((pieces, n_z)), dma((pieces, n_z)),
        dma((pieces, n_z, n_req)), dma((pieces, n_z, n_req)),
        dma((pieces, n_req)), dma((pieces, n_req)),
        dma((pieces,)), dma((pieces,)), dma((pieces, n_req)), dma((pieces, n_req)),
        dma((pieces, n_z)), dma((pieces, n_z)),
    ]
    hbm = pl.BlockSpec(memory_space=pl.ANY)
    return pl.pallas_call(
        functools.partial(kernel, n_req, n_mlp),
        name="layer",
        out_shape=jax.ShapeDtypeStruct((tp, width), BF16),
        in_specs=[hbm] * 18,
        out_specs=pl.BlockSpec(memory_space=pltpu.VMEM),
        scratch_shapes=scratch,
        compiler_params=pltpu.CompilerParams(
            collective_id=0, has_side_effects=True, vmem_limit_bytes=62 << 20),
    )(
        tokens, segments, owners, sink_keys, sink_values,
        attn_gain, post_attn_gain, ffn_gain, post_ffn_gain,
        window_keys, window_values, w_query, w_key, w_value, w_out, w_gate, w_up, w_down,
    )


def solution(mesh):
    both = P(("req", "mlp"), None)
    return jax.shard_map(
        functools.partial(shards, mesh.shape["req"], mesh.shape["mlp"]),
        mesh=mesh,
        in_specs=(
            both, P(), P(), P(None, "mlp"), P(None, "mlp"), P("req", "mlp"), P("req", "mlp"),
            P(), P(), P(), P(),
            P(None, "mlp"), P(None, "mlp"), P(None, "mlp"), P("mlp", None), both, both, both,
        ),
        out_specs=both,
        check_vma=False,
    )
```

```python
import functools
import math

import jax
import jax.numpy as jnp
from jax import lax
from jax.experimental import pallas as pl
from jax.experimental.pallas import tpu as pltpu
from jax.sharding import PartitionSpec as P

HD = 128
EPS = 1e-06
SOFT_CAP = 50.0
SCORE_SCALE = 1.0 / (12.0 * SOFT_CAP)
MESH = pl.DeviceIdType.MESH
F32 = jnp.float32
BF16 = jnp.bfloat16
NT = (((1,), (1,)), ((), ()))
GELU_C = math.sqrt(2.0 / math.pi)


def rms_scale(values):
    return values * lax.rsqrt(jnp.mean(values * values, axis=-1, keepdims=True) + EPS)


def weights_of(scores):
    return jnp.exp(SOFT_CAP * jnp.tanh(scores * SCORE_SCALE))


def chunks(total, size):
    return [(start, min(size, total - start)) for start in range(0, total, size)]


def kernel(
    n_req, n_mlp,
    tok_hbm, seg_hbm, own_hbm, sk_hbm, sv_hbm, gains_a, gains_pa, gains_f, gains_pf,
    wk_hbm, wv_hbm, wq_hbm, wkey_hbm, wval_hbm, wo_hbm, wg_hbm, wu_hbm, wd_hbm,
    out,
    tok, segments, owners, sink_k, sink_v,
    win_k, win_v, wq, wkey, wval, wo, stage, wg, wu, wd,
    attn_gain, post_attn_gain, ffn_gain, post_ffn_gain, load_sem,
    posv, segv,
    ag1, xr, qbuf, ekf, evf, psend, prec,
    pj, s1, r1, s3, r3, head_sum,
    ag2, xf, xb, hg, hu, hid, acc,
    t1, u1, t2, u2, t3f, t3, u3,
    ss_ag1z, rs_ag1z, ss_ag1c, rs_ag1c, ss_q, rs_q, ss_p, rs_p,
    ss_1, rs_1, ss_3, rs_3,
    ss_ag2z, rs_ag2z, ss_ag2r, rs_ag2r, ss_ag2c, rs_ag2c,
    ss_t1, rs_t1, ss_t2, rs_t2, ss_t3, rs_t3,
):
    n_z = n_mlp // 2
    rq = lax.axis_index("req")
    me = lax.axis_index("mlp")
    z = me // 2
    c = me % 2
    oc = 1 - c
    sib = z * 2 + oc
    tp, width = tok.shape
    group = tp * n_mlp
    span = n_z * tp
    total = group * n_req
    kv_cols = wkey.shape[1]
    q_cols = wq.shape[1]
    kv_heads = kv_cols // HD
    pieces, cols = ag2.shape[0], ag2.shape[-1]

    def z_other(step):
        index, weight = 0, 1
        while weight < n_z:
            bit = (z // weight) % 2
            index = index + weight * (1 - bit if step & weight else bit)
            weight *= 2
        return index

    def z_peer(step):
        return {"mlp": z_other(step) * 2 + c}

    def r_peer(step):
        return lax.rem(rq + step, n_req)

    z_far_first = list(range(n_z - 1, 0, -1))

    barrier = pltpu.get_barrier_semaphore()
    for step in z_far_first:
        pl.semaphore_signal(barrier, inc=1, device_id=z_peer(step), device_id_type=MESH)
    for step in range(1, n_req):
        pl.semaphore_signal(barrier, inc=1, device_id={"req": r_peer(step)}, device_id_type=MESH)
    pl.semaphore_signal(barrier, inc=1, device_id={"mlp": sib}, device_id_type=MESH)

    def lanes_of(j):
        return slice(j * cols, (j + 1) * cols)

    gate_loads = [
        (("g", j), wg_hbm.at[:, lanes_of(j)], stage.at[:, lanes_of(j)]) for j in range(pieces)]
    up_loads = [(("u", j), wu_hbm.at[:, lanes_of(j)], wd.at[:, lanes_of(j)]) for j in range(pieces)]
    turn_cols = math.gcd(384, cols)
    to_turn = [
        (name, raw, turned, start)
        for name, raw, turned in (("g", stage, wg), ("u", wd, wu))
        for start in range(0, width, turn_cols)]
    n_turns = len(to_turn)

    def turn(share):
        for _ in range(min(len(to_turn), max(1, n_turns * share // 24)) if share else len(to_turn)):
            name, raw, turned, start = to_turn.pop(0)
            if start % cols == 0:
                loads[name, start // cols].wait()
            turned[start:start + turn_cols, :] = raw[:, start:start + turn_cols].T

    loads = {}
    for number, (name, src, dst) in enumerate((
        ("tok", tok_hbm, tok), ("ga", gains_a, attn_gain.at[0]),
        ("seg", seg_hbm, segments), ("own", own_hbm, owners),
        *gate_loads[:2],
        ("q", wq_hbm, wq), ("k", wkey_hbm, wkey), ("v", wval_hbm, wval),
        ("sk", sk_hbm, sink_k), ("sv", sv_hbm, sink_v),
        ("wk", wk_hbm, win_k), ("wv", wv_hbm, win_v),
        *gate_loads[2:], *up_loads, ("o", wo_hbm, wo),
        ("gpa", gains_pa, post_attn_gain.at[0]), ("gf", gains_f, ffn_gain.at[0]),
        ("gpf", gains_pf, post_ffn_gain.at[0]),
        ("d", wd_hbm, wd),
    )):
        loads[name] = pltpu.make_async_copy(src, dst, load_sem.at[number])
        if name != "d":
            loads[name].start()

    sent = []

    def send(src, dst, send_sem, recv_sem, device):
        copy = pltpu.make_async_remote_copy(
            src_ref=src, dst_ref=dst, send_sem=send_sem, recv_sem=recv_sem,
            device_id=device, device_id_type=MESH,
        )
        copy.start()
        sent.append(copy)
        return copy

    def settle():
        for copy in sent:
            copy.wait_send()
        sent.clear()

    loads["tok"].wait()
    loads["ga"].wait()
    token_float = tok[...].astype(F32)
    ag1[c, z] = (rms_scale(token_float) * attn_gain[...]).astype(BF16)
    pl.semaphore_wait(barrier, n_z + n_req - 1)
    z_copies = {
        k: send(ag1.at[c, z], ag1.at[c, z], ss_ag1z.at[k], rs_ag1z.at[k], z_peer(k))
        for k in z_far_first
    }
    c_copies = [send(ag1.at[c, z], ag1.at[c, z], ss_ag1c.at[0], rs_ag1c.at[0], {"mlp": sib})]

    def row_of_token(t):
        device, inner = t // tp, t % tp
        return (device % 2) * span + (device // 2) * tp + inner

    loads["seg"].wait()
    loads["own"].wait()
    for g in range(n_req):
        at = jnp.int32(0)
        for t in range(group):
            if t:
                at = jnp.where(segments[g, t] == segments[g, t - 1], at + 1, 0)
            row = g * group + row_of_token(t)
            posv[row:row + 1, :] = jnp.full((1, HD), at, jnp.int32)
    extra = 2 * group
    column = lax.broadcasted_iota(jnp.int32, (group, extra), 1)
    row_at = lax.broadcasted_iota(jnp.int32, (group, extra), 0)
    seg_row = jnp.full((group, extra), -1, jnp.int32)
    column_token = jnp.full((group, extra), group, jnp.int32)
    row_token = jnp.zeros((group, extra), jnp.int32)
    for t in range(group):
        row = row_of_token(t)
        segv[row:row + 1, :] = jnp.full((1, extra), segments[rq, t], jnp.int32)
        seg_row = jnp.where(column == row, segments[rq, t], seg_row)
        column_token = jnp.where(column == row, t, column_token)
        row_token = jnp.where(row_at == row, t, row_token)
    n_sink = sink_k.shape[0]
    local = (segv[...] == seg_row) & (column_token <= row_token)
    sinks = (column >= group) & (column < group + n_sink)
    one = jnp.where(local | sinks, 1, 0)
    emask = jnp.concatenate([one, one], axis=0) > 0
    block_rows = win_k.shape[0]
    wpos = owners[rq] * block_rows + lax.broadcasted_iota(jnp.int32, (1, block_rows), 1)

    turn(4)
    for k in range(1, n_z):
        z_copies[k].wait_recv()
        block = ag1.at[c, z_other(k)]
        c_copies.append(send(block, block, ss_ag1c.at[k], rs_ag1c.at[k], {"mlp": sib}))
    for copy in c_copies:
        copy.wait_recv()
    for core in range(2):
        for level in range(n_z):
            row = core * span + level * tp
            xr[row:row + tp, :] = ag1[core, level].astype(F32)
    rows = xr[...].astype(BF16)

    loads["q"].wait()
    qbuf[rq] = jnp.dot(rows, wq[...], preferred_element_type=F32).astype(BF16)
    q_copies = [
        send(qbuf.at[rq], qbuf.at[rq], ss_q.at[k], rs_q.at[k], {"req": r_peer(k)})
        for k in range(1, n_req)
    ]
    loads["k"].wait()
    key_new = jnp.dot(rows, wkey[...], preferred_element_type=F32).astype(BF16)
    loads["v"].wait()
    value_new = jnp.dot(rows, wval[...], preferred_element_type=F32).astype(BF16)
    loads["sk"].wait()
    loads["sv"].wait()
    for target, new, sinks in ((ekf, key_new, sink_k), (evf, value_new, sink_v)):
        target[...] = jnp.zeros_like(target)
        target[0:group, :] = new.astype(F32)
        target[group:group + n_sink, :] = sinks[...].astype(F32)

    own_q = qbuf[rq]
    extra_k = ekf[...].astype(BF16)
    extra_v = evf[...].astype(BF16)
    own_num, own_den = [], []
    for j in range(kv_heads):
        lanes = slice(j * HD, (j + 1) * HD)
        pair = jnp.concatenate(
            [own_q[:, (2 * j + i) * HD:(2 * j + i + 1) * HD] for i in range(2)], axis=0)
        scores = lax.dot_general(pair, extra_k[:, lanes], NT, preferred_element_type=F32)
        weight = jnp.where(emask, weights_of(scores), 0.0)
        den = jnp.sum(weight, axis=-1, keepdims=True)
        num = jnp.dot(weight.astype(BF16), extra_v[:, lanes], preferred_element_type=F32)
        for i in range(2):
            own_num.append(num[i * group:(i + 1) * group])
            own_den.append(den[i * group:(i + 1) * group])

    visible = wpos > posv[:, 0:1]
    visible = jnp.where(visible, 1, 0)
    visible = jnp.concatenate([visible, visible], axis=0) > 0
    lane = lax.broadcasted_iota(jnp.int32, (total, HD), 1)
    loads["wk"].wait()
    loads["wv"].wait()
    turn(2)
    for copy in q_copies:
        copy.wait_recv()
    all_q = qbuf[...].reshape(total, q_cols)
    p_copies = {}
    for j in range(kv_heads):
        lanes = slice(j * HD, (j + 1) * HD)
        pair = jnp.concatenate(
            [all_q[:, (2 * j + i) * HD:(2 * j + i + 1) * HD] for i in range(2)], axis=0)
        scores = lax.dot_general(pair, win_k[:, lanes], NT, preferred_element_type=F32)
        weight = jnp.where(visible, weights_of(scores), 0.0)
        den = jnp.sum(weight, axis=-1, keepdims=True)
        num = jnp.dot(weight.astype(BF16), win_v[:, lanes], preferred_element_type=F32)
        dens = jnp.zeros((total, HD), F32)
        for i in range(2):
            rows_i = slice(i * total, (i + 1) * total)
            psend[:, j, :, i * HD:(i + 1) * HD] = num[rows_i].astype(BF16).reshape(n_req, group, HD)
            high = den[rows_i].astype(BF16).astype(F32)
            dens = jnp.where(lane == 2 * i, high, dens)
            dens = jnp.where(lane == 2 * i + 1, den[rows_i] - high, dens)
        psend[:, j, :, 2 * HD:] = dens.astype(BF16).reshape(n_req, group, HD)
        for k in range(1, n_req):
            p_copies[j, k] = send(
                psend.at[r_peer(k), j], prec.at[k - 1, j], ss_p.at[j, k], rs_p.at[j, k],
                {"req": r_peer(k)})
    turn(9)
    heads = []
    for j in range(kv_heads):
        partial = psend[rq, j].astype(F32)
        for k in range(1, n_req):
            p_copies[j, k].wait_recv()
            partial = partial + prec[k - 1, j].astype(F32)
        for i in range(2):
            num = own_num[2 * j + i] + partial[:, i * HD:(i + 1) * HD]
            base = 2 * HD + 2 * i
            den = own_den[2 * j + i] + partial[:, base:base + 1] + partial[:, base + 1:base + 2]
            heads.append((num / den).astype(BF16))
    attended = jnp.concatenate(heads, axis=1)

    loads["o"].wait()
    c_copies = []
    for j in range(pieces):
        pj[j] = jnp.dot(
            attended, wo[:, lanes_of(j)], preferred_element_type=F32).reshape(2, span, cols)
        s1[j] = pj[j, oc].astype(BF16)
        c_copies.append(send(s1.at[j], r1.at[j], ss_1.at[j], rs_1.at[j], {"mlp": sib}))
    z_copies = {}
    for j in range(pieces):
        c_copies[j].wait_recv()
        both = pj[j, c] + r1[j].astype(F32)
        for level in range(n_z):
            head_sum[j, level] = both[level * tp:(level + 1) * tp]
            s3[j, level] = both[level * tp:(level + 1) * tp].astype(BF16)
        for k in z_far_first:
            z_copies[j, k] = send(
                s3.at[j, z_other(k)], r3.at[j, k - 1], ss_3.at[j, k], rs_3.at[j, k], z_peer(k))
    for name in ("gpa", "gf", "gpf"):
        loads[name].wait()
    turn(0)
    loads["d"].start()
    projected, residual = [], []
    squares = jnp.zeros((tp, 1), F32)
    for j in range(pieces):
        total_j = head_sum[j, z]
        for k in range(1, n_z):
            z_copies[j, k].wait_recv()
            total_j = total_j + r3[j, k - 1].astype(F32)
        projected.append(total_j)
        squares = squares + jnp.sum(total_j * total_j, axis=-1, keepdims=True)
    scale = lax.rsqrt(squares / width + EPS)
    squares = jnp.zeros((tp, 1), F32)
    for j in range(pieces):
        part = token_float[:, lanes_of(j)] + projected[j] * scale * post_attn_gain[:, lanes_of(j)]
        residual.append(part)
        squares = squares + jnp.sum(part * part, axis=-1, keepdims=True)
    scale = lax.rsqrt(squares / width + EPS)

    z_copies, r_copies, c_copies = {}, {}, {}

    def spread(j, step):
        level = z_other(step)
        for k in range(1, n_req):
            r_copies[j, step, k] = send(
                ag2.at[j, 0, 0, level], ag2.at[j, 0, k, level], ss_ag2r.at[j, step, k],
                rs_ag2r.at[j, step, k], {"req": r_peer(k)})

    def cross(j, k):
        c_copies[j, k] = send(
            ag2.at[j, 0, k], ag2.at[j, 1, k], ss_ag2c.at[j, k], rs_ag2c.at[j, k], {"mlp": sib})

    def unpack(j, core, k):
        base = (core * n_req + k) * span
        for level in range(n_z):
            xf[base + level * tp:base + (level + 1) * tp, :] = ag2[j, core, k, level].astype(F32)

    for j in range(pieces):
        ag2[j, 0, 0, z] = (residual[j] * scale * ffn_gain[:, lanes_of(j)]).astype(BF16)
        for k in range(1, n_z):
            z_copies[j, k] = send(
                ag2.at[j, 0, 0, z], ag2.at[j, 0, 0, z], ss_ag2z.at[j, k], rs_ag2z.at[j, k],
                z_peer(k))
        spread(j, 0)
    for j in range(pieces):
        for step in range(1, n_z):
            z_copies[j, step].wait_recv()
            spread(j, step)
        cross(j, 0)

    def collect(j):
        for k in range(1, n_req):
            for step in range(n_z):
                r_copies[j, step, k].wait_recv()
            cross(j, k)

    collect(0)
    for j in range(pieces):
        for k in range(n_req):
            unpack(j, 0, k)
        for k in range(n_req):
            c_copies[j, k].wait_recv()
            unpack(j, 1, k)
        xb[...] = xf[...].astype(BF16)
        gate = jnp.dot(xb[...], wg[lanes_of(j), :], preferred_element_type=F32)
        if j:
            gate = gate + hg[...]
        hg[...] = gate
        if j + 1 < pieces:
            collect(j + 1)
        up = jnp.dot(xb[...], wu[lanes_of(j), :], preferred_element_type=F32)
        if j:
            up = up + hu[...]
        hu[...] = up
    gate = hg[...]
    inner = GELU_C * (gate + 0.044715 * (gate * gate * gate))
    hid[...] = (0.5 * gate * (1.0 + jnp.tanh(inner)) * hu[...]).astype(BF16)
    loads["d"].wait()

    first, second, third, finals = {}, {}, {}, []
    half = n_req * span
    for j in range(pieces):
        sums = jnp.dot(hid[...], wd[:, lanes_of(j)], preferred_element_type=F32)
        t1[j] = sums[half:].astype(BF16)
        acc[j] = sums[:half]
        first[j] = send(t1.at[j], u1.at[j], ss_t1.at[j], rs_t1.at[j], {"mlp": sib})
    for j in range(pieces):
        first[j].wait_recv()
        both = acc[j] + u1[j].astype(F32)
        for k in range(n_req - 1, 0, -1):
            t2[j, k] = both[k * span:(k + 1) * span].astype(BF16)
            second[j, k] = send(
                t2.at[j, k], u2.at[j, k], ss_t2.at[j, k], rs_t2.at[j, k],
                {"req": r_peer(n_req - k)})
        acc[j, 0:span] = both[:span]
    for j in range(pieces):
        both = acc[j, 0:span]
        for k in range(1, n_req):
            second[j, k].wait_recv()
            both = both + u2[j, k].astype(F32)
        for level in range(n_z):
            t3f[j, level] = both[level * tp:(level + 1) * tp]
            t3[j, level] = both[level * tp:(level + 1) * tp].astype(BF16)
        for k in z_far_first:
            third[j, k] = send(
                t3.at[j, z_other(k)], u3.at[j, k], ss_t3.at[j, k], rs_t3.at[j, k], z_peer(k))
    settle()
    squares = jnp.zeros((tp, 1), F32)
    for j in range(pieces):
        total_j = t3f[j, z]
        for k in range(1, n_z):
            third[j, k].wait_recv()
            total_j = total_j + u3[j, k].astype(F32)
        finals.append(total_j)
        squares = squares + jnp.sum(total_j * total_j, axis=-1, keepdims=True)
    scale = lax.rsqrt(squares / width + EPS)
    for j in range(pieces):
        out[:, lanes_of(j)] = (
            residual[j] + finals[j] * scale * post_ffn_gain[:, lanes_of(j)]).astype(BF16)


def shards(
    n_req, n_mlp,
    tokens, segments, owners, sink_keys, sink_values, window_keys, window_values,
    attn_gain, post_attn_gain, ffn_gain, post_ffn_gain,
    w_query, w_key, w_value, w_out, w_gate, w_up, w_down,
):
    tp, width = tokens.shape
    n_z = n_mlp // 2
    group = tp * n_mlp
    span = n_z * tp
    total = group * n_req
    q_cols, kv_cols, ff = w_query.shape[1], w_key.shape[1], w_gate.shape[0]
    kv_heads = kv_cols // HD
    extra = 2 * group
    pieces = 3 if n_req <= 4 else 1
    cols = width // pieces

    def v(shape, dtype=BF16):
        return pltpu.VMEM(shape, dtype)

    dma = pltpu.SemaphoreType.DMA
    scratch = [
        v(tokens.shape), pltpu.SMEM(segments.shape, jnp.int32), pltpu.SMEM(owners.shape, jnp.int32),
        v(sink_keys.shape), v(sink_values.shape)]
    scratch += [v(a.shape) for a in (
        window_keys, window_values, w_query, w_key, w_value, w_out, w_gate)]
    scratch += [v((width, ff)), v((width, ff)), v((ff, width))]
    scratch += [v((1, width), F32)] * 4
    scratch += [
        dma((16 + 2 * pieces,)),
        v((total, HD), jnp.int32), v((group, extra), jnp.int32),
        v((2, n_z, tp, width)), v((group, width), F32),
        v((n_req, group, q_cols)), v((extra, kv_cols), F32), v((extra, kv_cols), F32),
        v((n_req, kv_heads, group, 3 * HD)), v((n_req - 1, kv_heads, group, 3 * HD)),
        v((pieces, 2, span, cols), F32), v((pieces, span, cols)), v((pieces, span, cols)),
        v((pieces, n_z, tp, cols)), v((pieces, n_z - 1, tp, cols)),
        v((pieces, n_z, tp, cols), F32),
        v((pieces, 2, n_req, n_z, tp, cols)), v((total, cols), F32), v((total, cols)),
        v((total, ff), F32), v((total, ff), F32), v((total, ff)),
        v((pieces, n_req * span, cols), F32),
        v((pieces, n_req * span, cols)), v((pieces, n_req * span, cols)),
        v((pieces, n_req, span, cols)), v((pieces, n_req, span, cols)),
        v((pieces, n_z, tp, cols), F32), v((pieces, n_z, tp, cols)), v((pieces, n_z, tp, cols)),
        dma((n_z,)), dma((n_z,)), dma((n_z,)), dma((n_z,)),
        dma((n_req,)), dma((n_req,)), dma((kv_heads, n_req)), dma((kv_heads, n_req)),
        dma((pieces,)), dma((pieces,)), dma((pieces, n_z)), dma((pieces, n_z)),
        dma((pieces, n_z)), dma((pieces, n_z)),
        dma((pieces, n_z, n_req)), dma((pieces, n_z, n_req)),
        dma((pieces, n_req)), dma((pieces, n_req)),
        dma((pieces,)), dma((pieces,)), dma((pieces, n_req)), dma((pieces, n_req)),
        dma((pieces, n_z)), dma((pieces, n_z)),
    ]
    hbm = pl.BlockSpec(memory_space=pl.ANY)
    return pl.pallas_call(
        functools.partial(kernel, n_req, n_mlp),
        name="layer",
        out_shape=jax.ShapeDtypeStruct((tp, width), BF16),
        in_specs=[hbm] * 18,
        out_specs=pl.BlockSpec(memory_space=pltpu.VMEM),
        scratch_shapes=scratch,
        compiler_params=pltpu.CompilerParams(
            collective_id=0, has_side_effects=True, vmem_limit_bytes=62 << 20),
    )(
        tokens, segments, owners, sink_keys, sink_values,
        attn_gain, post_attn_gain, ffn_gain, post_ffn_gain,
        window_keys, window_values, w_query, w_key, w_value, w_out, w_gate, w_up, w_down,
    )


def solution(mesh):
    both = P(("req", "mlp"), None)
    return jax.shard_map(
        functools.partial(shards, mesh.shape["req"], mesh.shape["mlp"]),
        mesh=mesh,
        in_specs=(
            both, P(), P(), P(None, "mlp"), P(None, "mlp"), P("req", "mlp"), P("req", "mlp"),
            P(), P(), P(), P(),
            P(None, "mlp"), P(None, "mlp"), P(None, "mlp"), P("mlp", None), both, both, both,
        ),
        out_specs=both,
        check_vma=False,
    )
```

```python
import functools
import math

import jax
import jax.numpy as jnp
from jax import lax
from jax.experimental import pallas as pl
from jax.experimental.pallas import tpu as pltpu
from jax.sharding import PartitionSpec as P

HD = 128
EPS = 1e-06
SOFT_CAP = 50.0
SCORE_SCALE = 1.0 / (12.0 * SOFT_CAP)
MESH = pl.DeviceIdType.MESH
F32 = jnp.float32
BF16 = jnp.bfloat16
NT = (((1,), (1,)), ((), ()))
GELU_C = math.sqrt(2.0 / math.pi)


def rms_scale(values):
    return values * lax.rsqrt(jnp.mean(values * values, axis=-1, keepdims=True) + EPS)


def weights_of(scores):
    return jnp.exp(SOFT_CAP * jnp.tanh(scores * SCORE_SCALE))


def chunks(total, size):
    return [(start, min(size, total - start)) for start in range(0, total, size)]


def kernel(
    n_req, n_mlp,
    tok_hbm, seg_hbm, own_hbm, sk_hbm, sv_hbm, gains_a, gains_pa, gains_f, gains_pf,
    wk_hbm, wv_hbm, wq_hbm, wkey_hbm, wval_hbm, wo_hbm, wg_hbm, wu_hbm, wd_hbm,
    out,
    tok, segments, owners, sink_k, sink_v,
    win_k, win_v, wq, wkey, wval, wo, stage, wg, wu, wd,
    attn_gain, post_attn_gain, ffn_gain, post_ffn_gain, load_sem,
    posv, segv,
    ag1, xr, qbuf, ekf, evf, psend, prec,
    pj, s1, r1, s3, r3, head_sum,
    ag2, xf, hg, hu, hid, acc,
    t1, u1, t2, u2, t3f, t3, u3,
    ss_ag1z, rs_ag1z, ss_ag1c, rs_ag1c, ss_q, rs_q, ss_p, rs_p,
    ss_1, rs_1, ss_3, rs_3,
    ss_ag2z, rs_ag2z, ss_ag2r, rs_ag2r, ss_ag2c, rs_ag2c,
    ss_t1, rs_t1, ss_t2, rs_t2, ss_t3, rs_t3,
):
    n_z = n_mlp // 2
    rq = lax.axis_index("req")
    me = lax.axis_index("mlp")
    z = me // 2
    c = me % 2
    oc = 1 - c
    sib = z * 2 + oc
    tp, width = tok.shape
    group = tp * n_mlp
    span = n_z * tp
    total = group * n_req
    kv_cols = wkey.shape[1]
    q_cols = wq.shape[1]
    kv_heads = kv_cols // HD
    pieces, cols = ag2.shape[0], ag2.shape[-1]
    head_pieces, head_cols = pj.shape[0], pj.shape[-1]
    sum_pieces, sum_cols = acc.shape[0], acc.shape[-1]

    def z_other(step):
        index, weight = 0, 1
        while weight < n_z:
            bit = (z // weight) % 2
            index = index + weight * (1 - bit if step & weight else bit)
            weight *= 2
        return index

    def z_peer(step):
        return {"mlp": z_other(step) * 2 + c}

    def r_peer(step):
        return lax.rem(rq + step, n_req)

    z_far_first = list(range(n_z - 1, 0, -1))

    barrier = pltpu.get_barrier_semaphore()
    for step in z_far_first:
        pl.semaphore_signal(barrier, inc=1, device_id=z_peer(step), device_id_type=MESH)
    for step in range(1, n_req):
        pl.semaphore_signal(barrier, inc=1, device_id={"req": r_peer(step)}, device_id_type=MESH)
    pl.semaphore_signal(barrier, inc=1, device_id={"mlp": sib}, device_id_type=MESH)

    def lanes_of(j, size=cols):
        return slice(j * size, (j + 1) * size)

    gate_loads = [
        (("g", j), wg_hbm.at[:, lanes_of(j)], stage.at[:, lanes_of(j)]) for j in range(pieces)]
    up_loads = [(("u", j), wu_hbm.at[:, lanes_of(j)], wd.at[:, lanes_of(j)]) for j in range(pieces)]
    turn_cols = math.gcd(384, cols)
    to_turn = [
        (name, raw, turned, start)
        for name, raw, turned in (("g", stage, wg), ("u", wd, wu))
        for start in range(0, width, turn_cols)]
    n_turns = len(to_turn)

    def turn(share):
        for _ in range(min(len(to_turn), max(1, n_turns * share // 24)) if share else len(to_turn)):
            name, raw, turned, start = to_turn.pop(0)
            if start % cols == 0:
                loads[name, start // cols].wait()
            turned[start:start + turn_cols, :] = raw[:, start:start + turn_cols].T

    loads = {}
    for number, (name, src, dst) in enumerate((
        ("tok", tok_hbm, tok), ("ga", gains_a, attn_gain.at[0]),
        ("seg", seg_hbm, segments), ("own", own_hbm, owners),
        *gate_loads[:2],
        ("q", wq_hbm, wq), ("k", wkey_hbm, wkey), ("v", wval_hbm, wval),
        ("sk", sk_hbm, sink_k), ("sv", sv_hbm, sink_v),
        ("wk", wk_hbm, win_k), ("wv", wv_hbm, win_v),
        *gate_loads[2:], *up_loads, ("o", wo_hbm, wo),
        ("gpa", gains_pa, post_attn_gain.at[0]), ("gf", gains_f, ffn_gain.at[0]),
        ("gpf", gains_pf, post_ffn_gain.at[0]),
        ("d", wd_hbm, wd),
    )):
        loads[name] = pltpu.make_async_copy(src, dst, load_sem.at[number])
        if name != "d":
            loads[name].start()

    sent = []

    def send(src, dst, send_sem, recv_sem, device):
        copy = pltpu.make_async_remote_copy(
            src_ref=src, dst_ref=dst, send_sem=send_sem, recv_sem=recv_sem,
            device_id=device, device_id_type=MESH,
        )
        copy.start()
        sent.append(copy)
        return copy

    def settle():
        for copy in sent:
            copy.wait_send()
        sent.clear()

    loads["tok"].wait()
    loads["ga"].wait()
    token_float = tok[...].astype(F32)
    ag1[c, z] = (rms_scale(token_float) * attn_gain[...]).astype(BF16)
    pl.semaphore_wait(barrier, n_z + n_req - 1)
    z_copies = {
        k: send(ag1.at[c, z], ag1.at[c, z], ss_ag1z.at[k], rs_ag1z.at[k], z_peer(k))
        for k in z_far_first
    }
    c_copies = [send(ag1.at[c, z], ag1.at[c, z], ss_ag1c.at[0], rs_ag1c.at[0], {"mlp": sib})]

    def row_of_token(t):
        device, inner = t // tp, t % tp
        return (device % 2) * span + (device // 2) * tp + inner

    loads["seg"].wait()
    loads["own"].wait()
    for g in range(n_req):
        at = jnp.int32(0)
        for t in range(group):
            if t:
                at = jnp.where(segments[g, t] == segments[g, t - 1], at + 1, 0)
            row = g * group + row_of_token(t)
            posv[row:row + 1, :] = jnp.full((1, HD), at, jnp.int32)
    extra = 2 * group
    column = lax.broadcasted_iota(jnp.int32, (group, extra), 1)
    row_at = lax.broadcasted_iota(jnp.int32, (group, extra), 0)
    seg_row = jnp.full((group, extra), -1, jnp.int32)
    column_token = jnp.full((group, extra), group, jnp.int32)
    row_token = jnp.zeros((group, extra), jnp.int32)
    for t in range(group):
        row = row_of_token(t)
        segv[row:row + 1, :] = jnp.full((1, extra), segments[rq, t], jnp.int32)
        seg_row = jnp.where(column == row, segments[rq, t], seg_row)
        column_token = jnp.where(column == row, t, column_token)
        row_token = jnp.where(row_at == row, t, row_token)
    n_sink = sink_k.shape[0]
    local = (segv[...] == seg_row) & (column_token <= row_token)
    sinks = (column >= group) & (column < group + n_sink)
    one = jnp.where(local | sinks, 1, 0)
    emask = jnp.concatenate([one, one], axis=0) > 0
    block_rows = win_k.shape[0]
    wpos = owners[rq] * block_rows + lax.broadcasted_iota(jnp.int32, (1, block_rows), 1)

    turn(4)
    for k in range(1, n_z):
        z_copies[k].wait_recv()
        block = ag1.at[c, z_other(k)]
        c_copies.append(send(block, block, ss_ag1c.at[k], rs_ag1c.at[k], {"mlp": sib}))
    for copy in c_copies:
        copy.wait_recv()
    for core in range(2):
        for level in range(n_z):
            row = core * span + level * tp
            xr[row:row + tp, :] = ag1[core, level].astype(xr.dtype)
    rows = xr[...].astype(BF16)

    loads["q"].wait()
    qbuf[rq] = jnp.dot(rows, wq[...], preferred_element_type=F32).astype(BF16)
    q_copies = [
        send(qbuf.at[rq], qbuf.at[rq], ss_q.at[k], rs_q.at[k], {"req": r_peer(k)})
        for k in range(1, n_req)
    ]
    loads["k"].wait()
    key_new = jnp.dot(rows, wkey[...], preferred_element_type=F32).astype(BF16)
    loads["v"].wait()
    value_new = jnp.dot(rows, wval[...], preferred_element_type=F32).astype(BF16)
    loads["sk"].wait()
    loads["sv"].wait()
    for target, new, sinks in ((ekf, key_new, sink_k), (evf, value_new, sink_v)):
        target[...] = jnp.zeros_like(target)
        target[0:group, :] = new.astype(F32)
        target[group:group + n_sink, :] = sinks[...].astype(F32)

    own_q = qbuf[rq]
    extra_k = ekf[...].astype(BF16)
    extra_v = evf[...].astype(BF16)
    own_num, own_den = [], []
    for j in range(kv_heads):
        lanes = slice(j * HD, (j + 1) * HD)
        pair = jnp.concatenate(
            [own_q[:, (2 * j + i) * HD:(2 * j + i + 1) * HD] for i in range(2)], axis=0)
        scores = lax.dot_general(pair, extra_k[:, lanes], NT, preferred_element_type=F32)
        weight = jnp.where(emask, weights_of(scores), 0.0)
        den = jnp.sum(weight, axis=-1, keepdims=True)
        num = jnp.dot(weight.astype(BF16), extra_v[:, lanes], preferred_element_type=F32)
        for i in range(2):
            own_num.append(num[i * group:(i + 1) * group])
            own_den.append(den[i * group:(i + 1) * group])

    visible = wpos > posv[:, 0:1]
    visible = jnp.where(visible, 1, 0)
    visible = jnp.concatenate([visible, visible], axis=0) > 0
    lane = lax.broadcasted_iota(jnp.int32, (total, HD), 1)
    loads["wk"].wait()
    loads["wv"].wait()
    turn(2)
    for copy in q_copies:
        copy.wait_recv()
    all_q = qbuf[...].reshape(total, q_cols)
    p_copies = {}
    for j in range(kv_heads):
        lanes = slice(j * HD, (j + 1) * HD)
        pair = jnp.concatenate(
            [all_q[:, (2 * j + i) * HD:(2 * j + i + 1) * HD] for i in range(2)], axis=0)
        scores = lax.dot_general(pair, win_k[:, lanes], NT, preferred_element_type=F32)
        weight = jnp.where(visible, weights_of(scores), 0.0)
        den = jnp.sum(weight, axis=-1, keepdims=True)
        num = jnp.dot(weight.astype(BF16), win_v[:, lanes], preferred_element_type=F32)
        dens = jnp.zeros((total, HD), F32)
        for i in range(2):
            rows_i = slice(i * total, (i + 1) * total)
            psend[:, j, :, i * HD:(i + 1) * HD] = num[rows_i].astype(BF16).reshape(n_req, group, HD)
            high = den[rows_i].astype(BF16).astype(F32)
            dens = jnp.where(lane == 2 * i, high, dens)
            dens = jnp.where(lane == 2 * i + 1, den[rows_i] - high, dens)
        psend[:, j, :, 2 * HD:] = dens.astype(BF16).reshape(n_req, group, HD)
        for k in range(1, n_req):
            p_copies[j, k] = send(
                psend.at[r_peer(k), j], prec.at[k - 1, j], ss_p.at[j, k], rs_p.at[j, k],
                {"req": r_peer(k)})
    turn(9)
    heads = []
    for j in range(kv_heads):
        partial = psend[rq, j].astype(F32)
        for k in range(1, n_req):
            p_copies[j, k].wait_recv()
            partial = partial + prec[k - 1, j].astype(F32)
        for i in range(2):
            num = own_num[2 * j + i] + partial[:, i * HD:(i + 1) * HD]
            base = 2 * HD + 2 * i
            den = own_den[2 * j + i] + partial[:, base:base + 1] + partial[:, base + 1:base + 2]
            heads.append((num / den).astype(BF16))
    attended = jnp.concatenate(heads, axis=1)

    loads["o"].wait()
    c_copies = []
    for j in range(head_pieces):
        pj[j] = jnp.dot(
            attended, wo[:, lanes_of(j, head_cols)], preferred_element_type=F32).reshape(2, span, head_cols)
        s1[j] = pj[j, oc].astype(BF16)
        c_copies.append(send(s1.at[j], r1.at[j], ss_1.at[j], rs_1.at[j], {"mlp": sib}))
    z_copies = {}
    for j in range(head_pieces):
        c_copies[j].wait_recv()
        both = pj[j, c] + r1[j].astype(F32)
        for level in range(n_z):
            head_sum[j, level] = both[level * tp:(level + 1) * tp]
            s3[j, level] = both[level * tp:(level + 1) * tp].astype(BF16)
        for k in z_far_first:
            z_copies[j, k] = send(
                s3.at[j, z_other(k)], r3.at[j, k - 1], ss_3.at[j, k], rs_3.at[j, k], z_peer(k))
    for name in ("gpa", "gf", "gpf"):
        loads[name].wait()
    turn(0)
    loads["d"].start()
    projected, residual = [], []
    squares = jnp.zeros((tp, 1), F32)
    for j in range(head_pieces):
        total_j = head_sum[j, z]
        for k in range(1, n_z):
            z_copies[j, k].wait_recv()
            total_j = total_j + r3[j, k - 1].astype(F32)
        projected.append(total_j)
        squares = squares + jnp.sum(total_j * total_j, axis=-1, keepdims=True)
    scale = lax.rsqrt(squares / width + EPS)
    squares = jnp.zeros((tp, 1), F32)
    for j in range(head_pieces):
        part = token_float[:, lanes_of(j, head_cols)] + projected[j] * scale * post_attn_gain[:, lanes_of(j, head_cols)]
        residual.append(part)
        squares = squares + jnp.sum(part * part, axis=-1, keepdims=True)
    residual = jnp.concatenate(residual, axis=1)
    ffn_in = (residual * lax.rsqrt(squares / width + EPS) * ffn_gain[...]).astype(BF16)

    z_copies, r_copies, c_copies = {}, {}, {}

    def spread(j, step):
        level = z_other(step)
        for k in range(1, n_req):
            r_copies[j, step, k] = send(
                ag2.at[j, 0, 0, level], ag2.at[j, 0, k, level], ss_ag2r.at[j, step, k],
                rs_ag2r.at[j, step, k], {"req": r_peer(k)})

    def cross(j, k):
        c_copies[j, k] = send(
            ag2.at[j, 0, k], ag2.at[j, 1, k], ss_ag2c.at[j, k], rs_ag2c.at[j, k], {"mlp": sib})

    def unpack(j, core, k):
        base = (core * n_req + k) * span
        for level in range(n_z):
            xf[j, base + level * tp:base + (level + 1) * tp, :] = (
                ag2[j, core, k, level].astype(xf.dtype))

    for j in range(pieces):
        ag2[j, 0, 0, z] = ffn_in[:, lanes_of(j)]
        for k in range(1, n_z):
            z_copies[j, k] = send(
                ag2.at[j, 0, 0, z], ag2.at[j, 0, 0, z], ss_ag2z.at[j, k], rs_ag2z.at[j, k],
                z_peer(k))
        spread(j, 0)
    for j in range(pieces):
        for step in range(1, n_z):
            z_copies[j, step].wait_recv()
            spread(j, step)
        cross(j, 0)

    def collect(j):
        for k in range(1, n_req):
            for step in range(n_z):
                r_copies[j, step, k].wait_recv()
            cross(j, k)
            unpack(j, 0, k)

    for j in range(pieces):
        unpack(j, 0, 0)
    collect(0)
    for j in range(pieces):
        for k in range(n_req):
            c_copies[j, k].wait_recv()
            unpack(j, 1, k)
        x = xf[j].astype(BF16)
        gate = jnp.dot(x, wg[lanes_of(j), :], preferred_element_type=F32)
        if j:
            gate = gate + hg[...]
        hg[...] = gate
        if j + 1 < pieces:
            collect(j + 1)
        up = jnp.dot(x, wu[lanes_of(j), :], preferred_element_type=F32)
        if j:
            up = up + hu[...]
        hu[...] = up
    gate = hg[...]
    inner = GELU_C * (gate + 0.044715 * (gate * gate * gate))
    hid[...] = (0.5 * gate * (1.0 + jnp.tanh(inner)) * hu[...]).astype(BF16)
    loads["d"].wait()

    first, second, third, finals = {}, {}, {}, []
    half = n_req * span
    for j in range(sum_pieces):
        sums = jnp.dot(hid[...], wd[:, lanes_of(j, sum_cols)], preferred_element_type=F32)
        t1[j] = sums[half:].astype(BF16)
        acc[j] = sums[:half]
        first[j] = send(t1.at[j], u1.at[j], ss_t1.at[j], rs_t1.at[j], {"mlp": sib})
    for j in range(sum_pieces):
        first[j].wait_recv()
        both = acc[j] + u1[j].astype(F32)
        for k in range(n_req - 1, 0, -1):
            t2[j, k] = both[k * span:(k + 1) * span].astype(BF16)
            second[j, k] = send(
                t2.at[j, k], u2.at[j, k], ss_t2.at[j, k], rs_t2.at[j, k],
                {"req": r_peer(n_req - k)})
        acc[j, 0:span] = both[:span]
    for j in range(sum_pieces):
        both = acc[j, 0:span]
        for k in range(1, n_req):
            second[j, k].wait_recv()
            both = both + u2[j, k].astype(F32)
        for level in range(n_z):
            t3f[j, level] = both[level * tp:(level + 1) * tp]
            t3[j, level] = both[level * tp:(level + 1) * tp].astype(BF16)
        for k in z_far_first:
            third[j, k] = send(
                t3.at[j, z_other(k)], u3.at[j, k], ss_t3.at[j, k], rs_t3.at[j, k], z_peer(k))
    settle()
    squares = jnp.zeros((tp, 1), F32)
    for j in range(sum_pieces):
        total_j = t3f[j, z]
        for k in range(1, n_z):
            third[j, k].wait_recv()
            total_j = total_j + u3[j, k].astype(F32)
        finals.append(total_j)
        squares = squares + jnp.sum(total_j * total_j, axis=-1, keepdims=True)
    scale = lax.rsqrt(squares / width + EPS)
    for j in range(sum_pieces):
        out[:, lanes_of(j, sum_cols)] = (
            residual[:, lanes_of(j, sum_cols)] + finals[j] * scale * post_ffn_gain[:, lanes_of(j, sum_cols)]).astype(BF16)


def shards(
    n_req, n_mlp,
    tokens, segments, owners, sink_keys, sink_values, window_keys, window_values,
    attn_gain, post_attn_gain, ffn_gain, post_ffn_gain,
    w_query, w_key, w_value, w_out, w_gate, w_up, w_down,
):
    tp, width = tokens.shape
    n_z = n_mlp // 2
    group = tp * n_mlp
    span = n_z * tp
    total = group * n_req
    q_cols, kv_cols, ff = w_query.shape[1], w_key.shape[1], w_gate.shape[0]
    kv_heads = kv_cols // HD
    extra = 2 * group
    head_pieces, pieces, sum_pieces = (2, 2, 2) if n_req <= 4 else (1, 1, 1)
    head_cols, cols, sum_cols = width // head_pieces, width // pieces, width // sum_pieces

    rows_type = BF16 if tp % 2 == 0 else F32

    def v(shape, dtype=BF16):
        return pltpu.VMEM(shape, dtype)

    dma = pltpu.SemaphoreType.DMA
    scratch = [
        v(tokens.shape), pltpu.SMEM(segments.shape, jnp.int32), pltpu.SMEM(owners.shape, jnp.int32),
        v(sink_keys.shape), v(sink_values.shape)]
    scratch += [v(a.shape) for a in (
        window_keys, window_values, w_query, w_key, w_value, w_out, w_gate)]
    scratch += [v((width, ff)), v((width, ff)), v((ff, width))]
    scratch += [v((1, width), F32)] * 4
    scratch += [
        dma((16 + 2 * pieces,)),
        v((total, HD), jnp.int32), v((group, extra), jnp.int32),
        v((2, n_z, tp, width)), v((group, width), rows_type),
        v((n_req, group, q_cols)), v((extra, kv_cols), F32), v((extra, kv_cols), F32),
        v((n_req, kv_heads, group, 3 * HD)), v((n_req - 1, kv_heads, group, 3 * HD)),
        v((head_pieces, 2, span, head_cols), F32), v((head_pieces, span, head_cols)),
        v((head_pieces, span, head_cols)), v((head_pieces, n_z, tp, head_cols)),
        v((head_pieces, n_z - 1, tp, head_cols)), v((head_pieces, n_z, tp, head_cols), F32),
        v((pieces, 2, n_req, n_z, tp, cols)), v((pieces, total, cols), rows_type),
        v((total, ff), F32), v((total, ff), F32), v((total, ff)),
        v((sum_pieces, n_req * span, sum_cols), F32),
        v((sum_pieces, n_req * span, sum_cols)), v((sum_pieces, n_req * span, sum_cols)),
        v((sum_pieces, n_req, span, sum_cols)), v((sum_pieces, n_req, span, sum_cols)),
        v((sum_pieces, n_z, tp, sum_cols), F32), v((sum_pieces, n_z, tp, sum_cols)), v((sum_pieces, n_z, tp, sum_cols)),
        dma((n_z,)), dma((n_z,)), dma((n_z,)), dma((n_z,)),
        dma((n_req,)), dma((n_req,)), dma((kv_heads, n_req)), dma((kv_heads, n_req)),
        dma((head_pieces,)), dma((head_pieces,)), dma((head_pieces, n_z)), dma((head_pieces, n_z)),
        dma((pieces, n_z)), dma((pieces, n_z)),
        dma((pieces, n_z, n_req)), dma((pieces, n_z, n_req)),
        dma((pieces, n_req)), dma((pieces, n_req)),
        dma((sum_pieces,)), dma((sum_pieces,)), dma((sum_pieces, n_req)), dma((sum_pieces, n_req)),
        dma((sum_pieces, n_z)), dma((sum_pieces, n_z)),
    ]
    hbm = pl.BlockSpec(memory_space=pl.ANY)
    return pl.pallas_call(
        functools.partial(kernel, n_req, n_mlp),
        name="layer",
        out_shape=pltpu.VMEM((tp, width), BF16),
        in_specs=[hbm] * 18,
        out_specs=pl.BlockSpec(memory_space=pltpu.VMEM),
        scratch_shapes=scratch,
        compiler_params=pltpu.CompilerParams(
            collective_id=0, has_side_effects=True, vmem_limit_bytes=62 << 20),
    )(
        tokens, segments, owners, sink_keys, sink_values,
        attn_gain, post_attn_gain, ffn_gain, post_ffn_gain,
        window_keys, window_values, w_query, w_key, w_value, w_out, w_gate, w_up, w_down,
    )


def solution(mesh):
    both = P(("req", "mlp"), None)
    return jax.shard_map(
        functools.partial(shards, mesh.shape["req"], mesh.shape["mlp"]),
        mesh=mesh,
        in_specs=(
            both, P(), P(), P(None, "mlp"), P(None, "mlp"), P("req", "mlp"), P("req", "mlp"),
            P(), P(), P(), P(),
            P(None, "mlp"), P(None, "mlp"), P(None, "mlp"), P("mlp", None), both, both, both,
        ),
        out_specs=both,
        check_vma=False,
    )
```

```python
import functools
import math

import jax
import jax.numpy as jnp
from jax import lax
from jax.experimental import pallas as pl
from jax.experimental.pallas import tpu as pltpu
from jax.sharding import PartitionSpec as P

HD = 128
EPS = 1e-06
SOFT_CAP = 50.0
SCORE_SCALE = 1.0 / (12.0 * SOFT_CAP)
MESH = pl.DeviceIdType.MESH
F32 = jnp.float32
BF16 = jnp.bfloat16
NT = (((1,), (1,)), ((), ()))
GELU_C = math.sqrt(2.0 / math.pi)


def rms_scale(values):
    return values * lax.rsqrt(jnp.mean(values * values, axis=-1, keepdims=True) + EPS)


def weights_of(scores):
    return jnp.exp(SOFT_CAP * jnp.tanh(scores * SCORE_SCALE))


def chunks(total, size):
    return [(start, min(size, total - start)) for start in range(0, total, size)]


def kernel(
    n_req, n_mlp,
    tok_hbm, seg_hbm, own_hbm, sk_hbm, sv_hbm, gains_a, gains_pa, gains_f, gains_pf,
    wk_hbm, wv_hbm, wq_hbm, wkey_hbm, wval_hbm, wo_hbm, wg_hbm, wu_hbm, wd_hbm,
    out,
    tok, segments, owners, sink_k, sink_v,
    win_k, win_v, wq, wkey, wval, wo, stage, wg, wu, wd,
    attn_gain, post_attn_gain, ffn_gain, post_ffn_gain, load_sem,
    posv, segv,
    ag1, xr, qbuf, ekf, evf, psend, prec,
    pj, s1, r1, s3, r3, head_sum,
    ag2, xf, hg, hu, hid, acc,
    t1, u1, t2, u2, t3f, t3, u3, t4, u4,
    ss_ag1z, rs_ag1z, ss_ag1c, rs_ag1c, ss_q, rs_q, ss_p, rs_p,
    ss_1, rs_1, ss_3, rs_3,
    ss_ag2z, rs_ag2z, ss_ag2r, rs_ag2r, ss_ag2c, rs_ag2c,
    ss_t1, rs_t1, ss_t2, rs_t2, ss_t3, rs_t3, ss_t4, rs_t4,
):
    n_z = n_mlp // 2
    rq = lax.axis_index("req")
    me = lax.axis_index("mlp")
    z = me // 2
    c = me % 2
    oc = 1 - c
    sib = z * 2 + oc
    tp, width = tok.shape
    group = tp * n_mlp
    span = n_z * tp
    total = group * n_req
    kv_cols = wkey.shape[1]
    q_cols = wq.shape[1]
    kv_heads = kv_cols // HD
    pieces, cols = ag2.shape[0], ag2.shape[-1]
    head_pieces, head_cols = pj.shape[0], pj.shape[-1]
    sum_pieces, sum_cols = acc.shape[0], acc.shape[-1]

    def z_other(step):
        index, weight = 0, 1
        while weight < n_z:
            bit = (z // weight) % 2
            index = index + weight * (1 - bit if step & weight else bit)
            weight *= 2
        return index

    def z_peer(step):
        return {"mlp": z_other(step) * 2 + c}

    def r_peer(step):
        return lax.rem(rq + step, n_req)

    z_far_first = list(range(n_z - 1, 0, -1))
    far = n_z - 1
    at_edge = (z == 0) | (z == far)

    barrier = pltpu.get_barrier_semaphore()
    for step in z_far_first:
        pl.semaphore_signal(barrier, inc=1, device_id=z_peer(step), device_id_type=MESH)
    for step in range(1, n_req):
        pl.semaphore_signal(barrier, inc=1, device_id={"req": r_peer(step)}, device_id_type=MESH)
    pl.semaphore_signal(barrier, inc=1, device_id={"mlp": sib}, device_id_type=MESH)

    def lanes_of(j, size=cols):
        return slice(j * size, (j + 1) * size)

    gate_loads = [
        (("g", j), wg_hbm.at[:, lanes_of(j)], stage.at[:, lanes_of(j)]) for j in range(pieces)]
    up_loads = [(("u", j), wu_hbm.at[:, lanes_of(j)], wd.at[:, lanes_of(j)]) for j in range(pieces)]
    turn_cols = math.gcd(384, cols)
    to_turn = [
        (name, raw, turned, start)
        for name, raw, turned in (("g", stage, wg), ("u", wd, wu))
        for start in range(0, width, turn_cols)]
    n_turns = len(to_turn)

    def turn(share):
        for _ in range(min(len(to_turn), max(1, n_turns * share // 24)) if share else len(to_turn)):
            name, raw, turned, start = to_turn.pop(0)
            if start % cols == 0:
                loads[name, start // cols].wait()
            turned[start:start + turn_cols, :] = raw[:, start:start + turn_cols].T

    loads = {}
    for number, (name, src, dst) in enumerate((
        ("tok", tok_hbm, tok), ("ga", gains_a, attn_gain.at[0]),
        ("seg", seg_hbm, segments), ("own", own_hbm, owners),
        *gate_loads[:2],
        ("q", wq_hbm, wq), ("k", wkey_hbm, wkey), ("v", wval_hbm, wval),
        ("sk", sk_hbm, sink_k), ("sv", sv_hbm, sink_v),
        ("wk", wk_hbm, win_k), ("wv", wv_hbm, win_v),
        *gate_loads[2:], *up_loads, ("o", wo_hbm, wo),
        ("gpa", gains_pa, post_attn_gain.at[0]), ("gf", gains_f, ffn_gain.at[0]),
        ("gpf", gains_pf, post_ffn_gain.at[0]),
        ("d", wd_hbm, wd),
    )):
        loads[name] = pltpu.make_async_copy(src, dst, load_sem.at[number])
        if name != "d":
            loads[name].start()

    sent = []

    def send(src, dst, send_sem, recv_sem, device):
        copy = pltpu.make_async_remote_copy(
            src_ref=src, dst_ref=dst, send_sem=send_sem, recv_sem=recv_sem,
            device_id=device, device_id_type=MESH,
        )
        copy.start()
        sent.append(copy)
        return copy

    def send_if(wanted, *where):
        copy = pltpu.make_async_remote_copy(
            src_ref=where[0], dst_ref=where[1], send_sem=where[2], recv_sem=where[3],
            device_id=where[4], device_id_type=MESH)

        @pl.when(wanted)
        def _():
            copy.start()
        return copy

    def settle():
        for copy in sent:
            copy.wait_send()
        sent.clear()

    loads["tok"].wait()
    loads["ga"].wait()
    token_float = tok[...].astype(F32)
    ag1[c, z] = (rms_scale(token_float) * attn_gain[...]).astype(BF16)
    pl.semaphore_wait(barrier, n_z + n_req - 1)
    z_copies = {
        k: send(ag1.at[c, z], ag1.at[c, z], ss_ag1z.at[k], rs_ag1z.at[k], z_peer(k))
        for k in z_far_first
    }
    c_copies = [send(ag1.at[c, z], ag1.at[c, z], ss_ag1c.at[0], rs_ag1c.at[0], {"mlp": sib})]

    def row_of_token(t):
        device, inner = t // tp, t % tp
        return (device % 2) * span + (device // 2) * tp + inner

    loads["seg"].wait()
    loads["own"].wait()
    for g in range(n_req):
        at = jnp.int32(0)
        for t in range(group):
            if t:
                at = jnp.where(segments[g, t] == segments[g, t - 1], at + 1, 0)
            row = g * group + row_of_token(t)
            posv[row:row + 1, :] = jnp.full((1, HD), at, jnp.int32)
    extra = 2 * group
    column = lax.broadcasted_iota(jnp.int32, (group, extra), 1)
    row_at = lax.broadcasted_iota(jnp.int32, (group, extra), 0)
    seg_row = jnp.full((group, extra), -1, jnp.int32)
    column_token = jnp.full((group, extra), group, jnp.int32)
    row_token = jnp.zeros((group, extra), jnp.int32)
    for t in range(group):
        row = row_of_token(t)
        segv[row:row + 1, :] = jnp.full((1, extra), segments[rq, t], jnp.int32)
        seg_row = jnp.where(column == row, segments[rq, t], seg_row)
        column_token = jnp.where(column == row, t, column_token)
        row_token = jnp.where(row_at == row, t, row_token)
    n_sink = sink_k.shape[0]
    local = (segv[...] == seg_row) & (column_token <= row_token)
    sinks = (column >= group) & (column < group + n_sink)
    one = jnp.where(local | sinks, 1, 0)
    emask = jnp.concatenate([one, one], axis=0) > 0
    block_rows = win_k.shape[0]
    wpos = owners[rq] * block_rows + lax.broadcasted_iota(jnp.int32, (1, block_rows), 1)

    turn(4)
    for k in range(1, n_z):
        z_copies[k].wait_recv()
        block = ag1.at[c, z_other(k)]
        c_copies.append(send(block, block, ss_ag1c.at[k], rs_ag1c.at[k], {"mlp": sib}))
    for copy in c_copies:
        copy.wait_recv()
    for core in range(2):
        for level in range(n_z):
            row = core * span + level * tp
            xr[row:row + tp, :] = ag1[core, level].astype(xr.dtype)
    rows = xr[...].astype(BF16)

    loads["q"].wait()
    qbuf[rq] = jnp.dot(rows, wq[...], preferred_element_type=F32).astype(BF16)
    q_copies = [
        send(qbuf.at[rq], qbuf.at[rq], ss_q.at[k], rs_q.at[k], {"req": r_peer(k)})
        for k in range(1, n_req)
    ]
    loads["k"].wait()
    key_new = jnp.dot(rows, wkey[...], preferred_element_type=F32).astype(BF16)
    loads["v"].wait()
    value_new = jnp.dot(rows, wval[...], preferred_element_type=F32).astype(BF16)
    loads["sk"].wait()
    loads["sv"].wait()
    for target, new, sinks in ((ekf, key_new, sink_k), (evf, value_new, sink_v)):
        target[...] = jnp.zeros_like(target)
        target[0:group, :] = new.astype(F32)
        target[group:group + n_sink, :] = sinks[...].astype(F32)

    own_q = qbuf[rq]
    extra_k = ekf[...].astype(BF16)
    extra_v = evf[...].astype(BF16)
    own_num, own_den = [], []
    for j in range(kv_heads):
        lanes = slice(j * HD, (j + 1) * HD)
        pair = jnp.concatenate(
            [own_q[:, (2 * j + i) * HD:(2 * j + i + 1) * HD] for i in range(2)], axis=0)
        scores = lax.dot_general(pair, extra_k[:, lanes], NT, preferred_element_type=F32)
        weight = jnp.where(emask, weights_of(scores), 0.0)
        den = jnp.sum(weight, axis=-1, keepdims=True)
        num = jnp.dot(weight.astype(BF16), extra_v[:, lanes], preferred_element_type=F32)
        for i in range(2):
            own_num.append(num[i * group:(i + 1) * group])
            own_den.append(den[i * group:(i + 1) * group])

    visible = wpos > posv[:, 0:1]
    visible = jnp.where(visible, 1, 0)
    visible = jnp.concatenate([visible, visible], axis=0) > 0
    lane = lax.broadcasted_iota(jnp.int32, (total, HD), 1)
    loads["wk"].wait()
    loads["wv"].wait()
    turn(2)
    for copy in q_copies:
        copy.wait_recv()
    all_q = qbuf[...].reshape(total, q_cols)
    p_copies = {}
    for j in range(kv_heads):
        lanes = slice(j * HD, (j + 1) * HD)
        pair = jnp.concatenate(
            [all_q[:, (2 * j + i) * HD:(2 * j + i + 1) * HD] for i in range(2)], axis=0)
        scores = lax.dot_general(pair, win_k[:, lanes], NT, preferred_element_type=F32)
        weight = jnp.where(visible, weights_of(scores), 0.0)
        den = jnp.sum(weight, axis=-1, keepdims=True)
        num = jnp.dot(weight.astype(BF16), win_v[:, lanes], preferred_element_type=F32)
        dens = jnp.zeros((total, HD), F32)
        for i in range(2):
            rows_i = slice(i * total, (i + 1) * total)
            psend[:, j, :, i * HD:(i + 1) * HD] = num[rows_i].astype(BF16).reshape(n_req, group, HD)
            high = den[rows_i].astype(BF16).astype(F32)
            dens = jnp.where(lane == 2 * i, high, dens)
            dens = jnp.where(lane == 2 * i + 1, den[rows_i] - high, dens)
        psend[:, j, :, 2 * HD:] = dens.astype(BF16).reshape(n_req, group, HD)
        for k in range(1, n_req):
            p_copies[j, k] = send(
                psend.at[r_peer(k), j], prec.at[k - 1, j], ss_p.at[j, k], rs_p.at[j, k],
                {"req": r_peer(k)})
    turn(9)
    loads["o"].wait()
    c_copies = []
    for j in range(kv_heads):
        heads = []
        partial = psend[rq, j].astype(F32)
        for k in range(1, n_req):
            p_copies[j, k].wait_recv()
            partial = partial + prec[k - 1, j].astype(F32)
        for i in range(2):
            num = own_num[2 * j + i] + partial[:, i * HD:(i + 1) * HD]
            base = 2 * HD + 2 * i
            den = own_den[2 * j + i] + partial[:, base:base + 1] + partial[:, base + 1:base + 2]
            heads.append((num / den).astype(BF16))
        attended = jnp.concatenate(heads, axis=1)
        for i in range(head_pieces):
            product = jnp.dot(
                attended, wo[2 * j * HD:2 * (j + 1) * HD, lanes_of(i, head_cols)],
                preferred_element_type=F32).reshape(2, span, head_cols)
            pj[i] = pj[i] + product if j else product
            if j == kv_heads - 1:
                s1[i] = pj[i, oc].astype(BF16)
                c_copies.append(send(s1.at[i], r1.at[i], ss_1.at[i], rs_1.at[i], {"mlp": sib}))
    z_copies = {}
    for j in range(head_pieces):
        c_copies[j].wait_recv()
        both = pj[j, c] + r1[j].astype(F32)
        for level in range(n_z):
            head_sum[j, level] = both[level * tp:(level + 1) * tp]
            s3[j, level] = both[level * tp:(level + 1) * tp].astype(BF16)
        for k in z_far_first:
            z_copies[j, k] = send(
                s3.at[j, z_other(k)], r3.at[j, k - 1], ss_3.at[j, k], rs_3.at[j, k], z_peer(k))
    for name in ("gpa", "gf", "gpf"):
        loads[name].wait()
    turn(0)
    loads["d"].start()
    projected, residual = [], []
    squares = jnp.zeros((tp, 1), F32)
    for j in range(head_pieces):
        total_j = head_sum[j, z]
        for k in range(1, n_z):
            z_copies[j, k].wait_recv()
            total_j = total_j + r3[j, k - 1].astype(F32)
        projected.append(total_j)
        squares = squares + jnp.sum(total_j * total_j, axis=-1, keepdims=True)
    scale = lax.rsqrt(squares / width + EPS)
    squares = jnp.zeros((tp, 1), F32)
    for j in range(head_pieces):
        part = token_float[:, lanes_of(j, head_cols)] + projected[j] * scale * post_attn_gain[:, lanes_of(j, head_cols)]
        residual.append(part)
        squares = squares + jnp.sum(part * part, axis=-1, keepdims=True)
    residual = jnp.concatenate(residual, axis=1)
    ffn_in = (residual * lax.rsqrt(squares / width + EPS) * ffn_gain[...]).astype(BF16)

    z_copies, r_copies, c_copies = {}, {}, {}

    def spread(j, step):
        level = z_other(step)
        for k in range(1, n_req):
            where = (
                ag2.at[j, 0, 0, level], ag2.at[j, 0, k, level], ss_ag2r.at[j, step, k],
                rs_ag2r.at[j, step, k], {"req": r_peer(k)})
            if step == far:
                r_copies[j, step, k] = send_if(jnp.logical_not(at_edge), *where)
                sent.append(r_copies[j, step, k])
            else:
                r_copies[j, step, k] = send(*where)

    def spread_far(j):
        for k in range(1, n_req):
            send_if(
                at_edge, ag2.at[j, 0, 0, z], ag2.at[j, 0, k, z], ss_ag2r.at[j, far, k],
                rs_ag2r.at[j, far, k], {"req": r_peer(k), **z_peer(far)})

    def cross(j, k):
        c_copies[j, k] = send(
            ag2.at[j, 0, k], ag2.at[j, 1, k], ss_ag2c.at[j, k], rs_ag2c.at[j, k], {"mlp": sib})

    def unpack(j, core, k):
        base = (core * n_req + k) * span
        for level in range(n_z):
            xf[j, base + level * tp:base + (level + 1) * tp, :] = (
                ag2[j, core, k, level].astype(xf.dtype))

    for j in range(pieces):
        ag2[j, 0, 0, z] = ffn_in[:, lanes_of(j)]
        for k in range(1, n_z):
            z_copies[j, k] = send(
                ag2.at[j, 0, 0, z], ag2.at[j, 0, 0, z], ss_ag2z.at[j, k], rs_ag2z.at[j, k],
                z_peer(k))
        spread_far(j)
        spread(j, 0)
    for j in range(pieces):
        for step in range(1, n_z):
            z_copies[j, step].wait_recv()
            spread(j, step)
        cross(j, 0)

    def collect(j):
        for k in range(1, n_req):
            for step in range(n_z):
                r_copies[j, step, k].wait_recv()
            cross(j, k)
            unpack(j, 0, k)

    for j in range(pieces):
        unpack(j, 0, 0)
    collect(0)
    for j in range(pieces):
        for k in range(n_req):
            c_copies[j, k].wait_recv()
            unpack(j, 1, k)
        x = xf[j].astype(BF16)
        gate = jnp.dot(x, wg[lanes_of(j), :], preferred_element_type=F32)
        if j:
            gate = gate + hg[...]
        hg[...] = gate
        if j + 1 < pieces:
            collect(j + 1)
        up = jnp.dot(x, wu[lanes_of(j), :], preferred_element_type=F32)
        if j:
            up = up + hu[...]
        hu[...] = up
    gate = hg[...]
    inner = GELU_C * (gate + 0.044715 * (gate * gate * gate))
    hid[...] = (0.5 * gate * (1.0 + jnp.tanh(inner)) * hu[...]).astype(BF16)
    loads["d"].wait()

    first, second, third, finals = {}, {}, {}, []
    half = n_req * span
    straight = {}
    last = sum_pieces - 1
    for j in range(sum_pieces):
        sums = jnp.dot(hid[...], wd[:, lanes_of(j, sum_cols)], preferred_element_type=F32)
        t1[j] = sums[half:].astype(BF16)
        acc[j] = sums[:half]
        first[j] = send(t1.at[j], u1.at[j], ss_t1.at[j], rs_t1.at[j], {"mlp": sib})
    for j in range(sum_pieces):
        first[j].wait_recv()
        both = acc[j] + u1[j].astype(F32)
        if j == last:
            for k in range(n_req):
                for level in range(n_z):
                    row = k * span + level * tp
                    t4[k, level] = both[row:row + tp].astype(BF16)
            for level in range(n_z):
                t3f[j, level] = both[level * tp:(level + 1) * tp]
            for step in z_far_first + [0]:
                for k in range(n_req - 1, -1, -1):
                    if k or step:
                        straight[k, step] = send(
                            t4.at[k, z_other(step)], u4.at[k, step], ss_t4.at[k, step],
                            rs_t4.at[k, step], {"req": r_peer(n_req - k), **z_peer(step)})
            continue
        for k in range(n_req - 1, 0, -1):
            t2[j, k] = both[k * span:(k + 1) * span].astype(BF16)
            second[j, k] = send(
                t2.at[j, k], u2.at[j, k], ss_t2.at[j, k], rs_t2.at[j, k],
                {"req": r_peer(n_req - k)})
        acc[j, 0:span] = both[:span]
    for j in range(last):
        both = acc[j, 0:span]
        for k in range(1, n_req):
            second[j, k].wait_recv()
            both = both + u2[j, k].astype(F32)
        for level in range(n_z):
            t3f[j, level] = both[level * tp:(level + 1) * tp]
            t3[j, level] = both[level * tp:(level + 1) * tp].astype(BF16)
        for k in z_far_first:
            third[j, k] = send(
                t3.at[j, z_other(k)], u3.at[j, k], ss_t3.at[j, k], rs_t3.at[j, k], z_peer(k))
    settle()
    squares = jnp.zeros((tp, 1), F32)
    for j in range(sum_pieces):
        total_j = t3f[j, z]
        for (k, step), copy in straight.items() if j == last else ():
            copy.wait_recv()
            total_j = total_j + u4[k, step].astype(F32)
        for k in range(1, n_z) if j < last else ():
            third[j, k].wait_recv()
            total_j = total_j + u3[j, k].astype(F32)
        finals.append(total_j)
        squares = squares + jnp.sum(total_j * total_j, axis=-1, keepdims=True)
    scale = lax.rsqrt(squares / width + EPS)
    for j in range(sum_pieces):
        out[:, lanes_of(j, sum_cols)] = (
            residual[:, lanes_of(j, sum_cols)] + finals[j] * scale * post_ffn_gain[:, lanes_of(j, sum_cols)]).astype(BF16)


def shards(
    n_req, n_mlp,
    tokens, segments, owners, sink_keys, sink_values, window_keys, window_values,
    attn_gain, post_attn_gain, ffn_gain, post_ffn_gain,
    w_query, w_key, w_value, w_out, w_gate, w_up, w_down,
):
    tp, width = tokens.shape
    n_z = n_mlp // 2
    group = tp * n_mlp
    span = n_z * tp
    total = group * n_req
    q_cols, kv_cols, ff = w_query.shape[1], w_key.shape[1], w_gate.shape[0]
    kv_heads = kv_cols // HD
    extra = 2 * group
    head_pieces, pieces, sum_pieces = (2, 2, 2) if n_req <= 4 else (1, 1, 1)
    head_cols, cols, sum_cols = width // head_pieces, width // pieces, width // sum_pieces

    rows_type = BF16 if tp % 2 == 0 else F32

    def v(shape, dtype=BF16):
        return pltpu.VMEM(shape, dtype)

    dma = pltpu.SemaphoreType.DMA
    scratch = [
        v(tokens.shape), pltpu.SMEM(segments.shape, jnp.int32), pltpu.SMEM(owners.shape, jnp.int32),
        v(sink_keys.shape), v(sink_values.shape)]
    scratch += [v(a.shape) for a in (
        window_keys, window_values, w_query, w_key, w_value, w_out, w_gate)]
    scratch += [v((width, ff)), v((width, ff)), v((ff, width))]
    scratch += [v((1, width), F32)] * 4
    scratch += [
        dma((16 + 2 * pieces,)),
        v((total, HD), jnp.int32), v((group, extra), jnp.int32),
        v((2, n_z, tp, width)), v((group, width), rows_type),
        v((n_req, group, q_cols)), v((extra, kv_cols), F32), v((extra, kv_cols), F32),
        v((n_req, kv_heads, group, 3 * HD)), v((n_req - 1, kv_heads, group, 3 * HD)),
        v((head_pieces, 2, span, head_cols), F32), v((head_pieces, span, head_cols)),
        v((head_pieces, span, head_cols)), v((head_pieces, n_z, tp, head_cols)),
        v((head_pieces, n_z - 1, tp, head_cols)), v((head_pieces, n_z, tp, head_cols), F32),
        v((pieces, 2, n_req, n_z, tp, cols)), v((pieces, total, cols), rows_type),
        v((total, ff), F32), v((total, ff), F32), v((total, ff)),
        v((sum_pieces, n_req * span, sum_cols), F32),
        v((sum_pieces, n_req * span, sum_cols)), v((sum_pieces, n_req * span, sum_cols)),
        v((sum_pieces, n_req, span, sum_cols)), v((sum_pieces, n_req, span, sum_cols)),
        v((sum_pieces, n_z, tp, sum_cols), F32), v((sum_pieces, n_z, tp, sum_cols)), v((sum_pieces, n_z, tp, sum_cols)),
        v((n_req, n_z, tp, sum_cols)), v((n_req, n_z, tp, sum_cols)),
        dma((n_z,)), dma((n_z,)), dma((n_z,)), dma((n_z,)),
        dma((n_req,)), dma((n_req,)), dma((kv_heads, n_req)), dma((kv_heads, n_req)),
        dma((head_pieces,)), dma((head_pieces,)), dma((head_pieces, n_z)), dma((head_pieces, n_z)),
        dma((pieces, n_z)), dma((pieces, n_z)),
        dma((pieces, n_z, n_req)), dma((pieces, n_z, n_req)),
        dma((pieces, n_req)), dma((pieces, n_req)),
        dma((sum_pieces,)), dma((sum_pieces,)), dma((sum_pieces, n_req)), dma((sum_pieces, n_req)),
        dma((sum_pieces, n_z)), dma((sum_pieces, n_z)), dma((n_req, n_z)), dma((n_req, n_z)),
    ]
    hbm = pl.BlockSpec(memory_space=pl.ANY)
    return pl.pallas_call(
        functools.partial(kernel, n_req, n_mlp),
        name="layer",
        out_shape=pltpu.VMEM((tp, width), BF16),
        in_specs=[hbm] * 18,
        out_specs=pl.BlockSpec(memory_space=pltpu.VMEM),
        scratch_shapes=scratch,
        compiler_params=pltpu.CompilerParams(
            collective_id=0, has_side_effects=True, vmem_limit_bytes=62 << 20),
    )(
        tokens, segments, owners, sink_keys, sink_values,
        attn_gain, post_attn_gain, ffn_gain, post_ffn_gain,
        window_keys, window_values, w_query, w_key, w_value, w_out, w_gate, w_up, w_down,
    )


def solution(mesh):
    both = P(("req", "mlp"), None)
    return jax.shard_map(
        functools.partial(shards, mesh.shape["req"], mesh.shape["mlp"]),
        mesh=mesh,
        in_specs=(
            both, P(), P(), P(None, "mlp"), P(None, "mlp"), P("req", "mlp"), P("req", "mlp"),
            P(), P(), P(), P(),
            P(None, "mlp"), P(None, "mlp"), P(None, "mlp"), P("mlp", None), both, both, both,
        ),
        out_specs=both,
        check_vma=False,
    )
```

```python
import functools
import math

import jax
import jax.numpy as jnp
from jax import lax
from jax.experimental import pallas as pl
from jax.experimental.pallas import tpu as pltpu
from jax.sharding import PartitionSpec as P

HD = 128
EPS = 1e-06
SOFT_CAP = 50.0
SCORE_SCALE = 1.0 / (12.0 * SOFT_CAP)
MESH = pl.DeviceIdType.MESH
F32 = jnp.float32
BF16 = jnp.bfloat16
NT = (((1,), (1,)), ((), ()))
GELU_C = math.sqrt(2.0 / math.pi)


def rms_scale(values):
    return values * lax.rsqrt(jnp.mean(values * values, axis=-1, keepdims=True) + EPS)


def weights_of(scores):
    return jnp.exp(SOFT_CAP * jnp.tanh(scores * SCORE_SCALE))


def chunks(total, size):
    return [(start, min(size, total - start)) for start in range(0, total, size)]


def kernel(
    n_req, n_mlp,
    tok_hbm, seg_hbm, own_hbm, sk_hbm, sv_hbm, gains_a, gains_pa, gains_f, gains_pf,
    wk_hbm, wv_hbm, wq_hbm, wkey_hbm, wval_hbm, wo_hbm, wg_hbm, wu_hbm, wd_hbm,
    out,
    tok, segments, owners, sink_k, sink_v,
    win_k, win_v, wq, wkey, wval, wo, stage, wg, wu, wd,
    attn_gain, post_attn_gain, ffn_gain, post_ffn_gain, load_sem,
    posv, segv,
    ag1, xr, qbuf, ekf, evf, psend, prec,
    pj, s1, r1, s3, r3, head_sum,
    ag2, xf, hg, hu, hid, acc,
    t1, u1, t2, u2, t3f, t3, u3, t4, u4,
    ss_ag1z, rs_ag1z, ss_ag1c, rs_ag1c, ss_q, rs_q, ss_p, rs_p,
    ss_1, rs_1, ss_3, rs_3,
    ss_ag2z, rs_ag2z, ss_ag2r, rs_ag2r, ss_ag2c, rs_ag2c,
    ss_t1, rs_t1, ss_t2, rs_t2, ss_t3, rs_t3, ss_t4, rs_t4,
):
    n_z = n_mlp // 2
    rq = lax.axis_index("req")
    me = lax.axis_index("mlp")
    z = me // 2
    c = me % 2
    oc = 1 - c
    sib = z * 2 + oc
    tp, width = tok.shape
    group = tp * n_mlp
    span = n_z * tp
    total = group * n_req
    kv_cols = wkey.shape[1]
    q_cols = wq.shape[1]
    kv_heads = kv_cols // HD
    pieces, cols = ag2.shape[0], ag2.shape[-1]
    head_pieces, head_cols = pj.shape[0], pj.shape[-1]
    sum_pieces, sum_cols = acc.shape[0], acc.shape[-1]

    def z_other(step):
        index, weight = 0, 1
        while weight < n_z:
            bit = (z // weight) % 2
            index = index + weight * (1 - bit if step & weight else bit)
            weight *= 2
        return index

    def z_peer(step):
        return {"mlp": z_other(step) * 2 + c}

    def r_peer(step):
        return lax.rem(rq + step, n_req)

    z_far_first = list(range(n_z - 1, 0, -1))
    far = n_z - 1
    at_edge = (z == 0) | (z == far)

    barrier = pltpu.get_barrier_semaphore()
    for step in z_far_first:
        pl.semaphore_signal(barrier, inc=1, device_id=z_peer(step), device_id_type=MESH)
    for step in range(1, n_req):
        pl.semaphore_signal(barrier, inc=1, device_id={"req": r_peer(step)}, device_id_type=MESH)
    pl.semaphore_signal(barrier, inc=1, device_id={"mlp": sib}, device_id_type=MESH)

    def lanes_of(j, size=cols):
        return slice(j * size, (j + 1) * size)

    gate_loads = [
        (("g", j), wg_hbm.at[:, lanes_of(j)], stage.at[:, lanes_of(j)]) for j in range(pieces)]
    up_loads = [(("u", j), wu_hbm.at[:, lanes_of(j)], wd.at[:, lanes_of(j)]) for j in range(pieces)]
    turn_cols = math.gcd(384, cols)
    to_turn = [
        (name, raw, turned, start)
        for name, raw, turned in (("g", stage, wg), ("u", wd, wu))
        for start in range(0, width, turn_cols)]
    n_turns = len(to_turn)

    def turn(share):
        for _ in range(min(len(to_turn), max(1, n_turns * share // 24)) if share else len(to_turn)):
            name, raw, turned, start = to_turn.pop(0)
            if start % cols == 0:
                loads[name, start // cols].wait()
            turned[start:start + turn_cols, :] = raw[:, start:start + turn_cols].T

    loads = {}
    for number, (name, src, dst) in enumerate((
        ("tok", tok_hbm, tok), ("ga", gains_a, attn_gain.at[0]),
        ("seg", seg_hbm, segments), ("own", own_hbm, owners),
        *gate_loads[:2],
        ("q", wq_hbm, wq), ("k", wkey_hbm, wkey), ("v", wval_hbm, wval),
        ("sk", sk_hbm, sink_k), ("sv", sv_hbm, sink_v),
        ("wk", wk_hbm, win_k), ("wv", wv_hbm, win_v),
        *gate_loads[2:], *up_loads, ("o", wo_hbm, wo),
        ("gpa", gains_pa, post_attn_gain.at[0]), ("gf", gains_f, ffn_gain.at[0]),
        ("gpf", gains_pf, post_ffn_gain.at[0]),
        ("d", wd_hbm, wd),
    )):
        loads[name] = pltpu.make_async_copy(src, dst, load_sem.at[number])
        if name != "d":
            loads[name].start()

    sent = []

    def send(src, dst, send_sem, recv_sem, device):
        copy = pltpu.make_async_remote_copy(
            src_ref=src, dst_ref=dst, send_sem=send_sem, recv_sem=recv_sem,
            device_id=device, device_id_type=MESH,
        )
        copy.start()
        sent.append(copy)
        return copy

    def send_if(wanted, *where):
        copy = pltpu.make_async_remote_copy(
            src_ref=where[0], dst_ref=where[1], send_sem=where[2], recv_sem=where[3],
            device_id=where[4], device_id_type=MESH)

        @pl.when(wanted)
        def _():
            copy.start()
        return copy

    def settle():
        for copy in sent:
            copy.wait_send()
        sent.clear()

    loads["tok"].wait()
    loads["ga"].wait()
    token_float = tok[...].astype(F32)
    ag1[c, z] = (rms_scale(token_float) * attn_gain[...]).astype(BF16)
    pl.semaphore_wait(barrier, n_z + n_req - 1)
    z_copies = {
        k: send(ag1.at[c, z], ag1.at[c, z], ss_ag1z.at[k], rs_ag1z.at[k], z_peer(k))
        for k in z_far_first
    }
    c_copies = [send(ag1.at[c, z], ag1.at[c, z], ss_ag1c.at[0], rs_ag1c.at[0], {"mlp": sib})]

    def row_of_token(t):
        device, inner = t // tp, t % tp
        return (device % 2) * span + (device // 2) * tp + inner

    loads["seg"].wait()
    loads["own"].wait()
    for g in range(n_req):
        at = jnp.int32(0)
        for t in range(group):
            if t:
                at = jnp.where(segments[g, t] == segments[g, t - 1], at + 1, 0)
            row = g * group + row_of_token(t)
            posv[row:row + 1, :] = jnp.full((1, HD), at, jnp.int32)
    extra = 2 * group
    column = lax.broadcasted_iota(jnp.int32, (group, extra), 1)
    row_at = lax.broadcasted_iota(jnp.int32, (group, extra), 0)
    seg_row = jnp.full((group, extra), -1, jnp.int32)
    column_token = jnp.full((group, extra), group, jnp.int32)
    row_token = jnp.zeros((group, extra), jnp.int32)
    for t in range(group):
        row = row_of_token(t)
        segv[row:row + 1, :] = jnp.full((1, extra), segments[rq, t], jnp.int32)
        seg_row = jnp.where(column == row, segments[rq, t], seg_row)
        column_token = jnp.where(column == row, t, column_token)
        row_token = jnp.where(row_at == row, t, row_token)
    n_sink = sink_k.shape[0]
    local = (segv[...] == seg_row) & (column_token <= row_token)
    sinks = (column >= group) & (column < group + n_sink)
    one = jnp.where(local | sinks, 1, 0)
    emask = jnp.concatenate([one, one], axis=0) > 0
    block_rows = win_k.shape[0]
    wpos = owners[rq] * block_rows + lax.broadcasted_iota(jnp.int32, (1, block_rows), 1)

    turn(4)
    for k in range(1, n_z):
        z_copies[k].wait_recv()
        block = ag1.at[c, z_other(k)]
        c_copies.append(send(block, block, ss_ag1c.at[k], rs_ag1c.at[k], {"mlp": sib}))
    for copy in c_copies:
        copy.wait_recv()
    for core in range(2):
        for level in range(n_z):
            row = core * span + level * tp
            xr[row:row + tp, :] = ag1[core, level].astype(xr.dtype)
    rows = xr[...].astype(BF16)

    loads["q"].wait()
    qbuf[rq] = jnp.dot(rows, wq[...], preferred_element_type=F32).astype(BF16)
    q_copies = [
        send(qbuf.at[rq], qbuf.at[rq], ss_q.at[k], rs_q.at[k], {"req": r_peer(k)})
        for k in range(1, n_req)
    ]
    loads["k"].wait()
    key_new = jnp.dot(rows, wkey[...], preferred_element_type=F32).astype(BF16)
    loads["v"].wait()
    value_new = jnp.dot(rows, wval[...], preferred_element_type=F32).astype(BF16)
    loads["sk"].wait()
    loads["sv"].wait()
    for target, new, sinks in ((ekf, key_new, sink_k), (evf, value_new, sink_v)):
        target[...] = jnp.zeros_like(target)
        target[0:group, :] = new.astype(F32)
        target[group:group + n_sink, :] = sinks[...].astype(F32)

    own_q = qbuf[rq]
    extra_k = ekf[...].astype(BF16)
    extra_v = evf[...].astype(BF16)
    own_num, own_den = [], []
    for j in range(kv_heads):
        lanes = slice(j * HD, (j + 1) * HD)
        pair = jnp.concatenate(
            [own_q[:, (2 * j + i) * HD:(2 * j + i + 1) * HD] for i in range(2)], axis=0)
        scores = lax.dot_general(pair, extra_k[:, lanes], NT, preferred_element_type=F32)
        weight = jnp.where(emask, weights_of(scores), 0.0)
        den = jnp.sum(weight, axis=-1, keepdims=True)
        num = jnp.dot(weight.astype(BF16), extra_v[:, lanes], preferred_element_type=F32)
        for i in range(2):
            own_num.append(num[i * group:(i + 1) * group])
            own_den.append(den[i * group:(i + 1) * group])

    visible = wpos > posv[:, 0:1]
    visible = jnp.where(visible, 1, 0)
    visible = jnp.concatenate([visible, visible], axis=0) > 0
    lane = lax.broadcasted_iota(jnp.int32, (total, HD), 1)
    loads["wk"].wait()
    loads["wv"].wait()
    turn(2)
    for copy in q_copies:
        copy.wait_recv()
    all_q = qbuf[...].reshape(total, q_cols)
    p_copies = {}
    for j in range(kv_heads):
        lanes = slice(j * HD, (j + 1) * HD)
        pair = jnp.concatenate(
            [all_q[:, (2 * j + i) * HD:(2 * j + i + 1) * HD] for i in range(2)], axis=0)
        scores = lax.dot_general(pair, win_k[:, lanes], NT, preferred_element_type=F32)
        weight = jnp.where(visible, weights_of(scores), 0.0)
        den = jnp.sum(weight, axis=-1, keepdims=True)
        num = jnp.dot(weight.astype(BF16), win_v[:, lanes], preferred_element_type=F32)
        dens = jnp.zeros((total, HD), F32)
        for i in range(2):
            rows_i = slice(i * total, (i + 1) * total)
            psend[:, j, :, i * HD:(i + 1) * HD] = num[rows_i].astype(BF16).reshape(n_req, group, HD)
            high = den[rows_i].astype(BF16).astype(F32)
            dens = jnp.where(lane == 2 * i, high, dens)
            dens = jnp.where(lane == 2 * i + 1, den[rows_i] - high, dens)
        psend[:, j, :, 2 * HD:] = dens.astype(BF16).reshape(n_req, group, HD)
        for k in range(1, n_req):
            p_copies[j, k] = send(
                psend.at[r_peer(k), j], prec.at[k - 1, j], ss_p.at[j, k], rs_p.at[j, k],
                {"req": r_peer(k)})
    turn(9)
    loads["o"].wait()
    c_copies = []
    for j in range(kv_heads):
        heads = []
        partial = psend[rq, j].astype(F32)
        for k in range(1, n_req):
            p_copies[j, k].wait_recv()
            partial = partial + prec[k - 1, j].astype(F32)
        for i in range(2):
            num = own_num[2 * j + i] + partial[:, i * HD:(i + 1) * HD]
            base = 2 * HD + 2 * i
            den = own_den[2 * j + i] + partial[:, base:base + 1] + partial[:, base + 1:base + 2]
            heads.append((num / den).astype(BF16))
        attended = jnp.concatenate(heads, axis=1)
        for i in range(head_pieces):
            product = jnp.dot(
                attended, wo[2 * j * HD:2 * (j + 1) * HD, lanes_of(i, head_cols)],
                preferred_element_type=F32).reshape(2, span, head_cols)
            pj[i] = pj[i] + product if j else product
            if j == kv_heads - 1:
                s1[i] = pj[i, oc].astype(BF16)
                c_copies.append(send(s1.at[i], r1.at[i], ss_1.at[i], rs_1.at[i], {"mlp": sib}))
    z_copies = {}
    for j in range(head_pieces):
        c_copies[j].wait_recv()
        both = pj[j, c] + r1[j].astype(F32)
        for level in range(n_z):
            head_sum[j, level] = both[level * tp:(level + 1) * tp]
            s3[j, level] = both[level * tp:(level + 1) * tp].astype(BF16)
        for k in z_far_first:
            z_copies[j, k] = send(
                s3.at[j, z_other(k)], r3.at[j, k - 1], ss_3.at[j, k], rs_3.at[j, k], z_peer(k))
    for name in ("gpa", "gf", "gpf"):
        loads[name].wait()
    turn(0)
    loads["d"].start()
    projected, residual = [], []
    squares = jnp.zeros((tp, 1), F32)
    for j in range(head_pieces):
        total_j = head_sum[j, z]
        for k in range(1, n_z):
            z_copies[j, k].wait_recv()
            total_j = total_j + r3[j, k - 1].astype(F32)
        projected.append(total_j)
        squares = squares + jnp.sum(total_j * total_j, axis=-1, keepdims=True)
    scale = lax.rsqrt(squares / width + EPS)
    squares = jnp.zeros((tp, 1), F32)
    for j in range(head_pieces):
        part = token_float[:, lanes_of(j, head_cols)] + projected[j] * scale * post_attn_gain[:, lanes_of(j, head_cols)]
        residual.append(part)
        squares = squares + jnp.sum(part * part, axis=-1, keepdims=True)
    residual = jnp.concatenate(residual, axis=1)
    ffn_in = (residual * lax.rsqrt(squares / width + EPS) * ffn_gain[...]).astype(BF16)

    z_copies, r_copies, c_copies = {}, {}, {}

    def spread(j, step):
        level = z_other(step)
        for k in range(1, n_req):
            where = (
                ag2.at[j, 0, 0, level], ag2.at[j, 0, k, level], ss_ag2r.at[j, step, k],
                rs_ag2r.at[j, step, k], {"req": r_peer(k)})
            if step == far:
                r_copies[j, step, k] = send_if(jnp.logical_not(at_edge), *where)
                sent.append(r_copies[j, step, k])
            else:
                r_copies[j, step, k] = send(*where)

    def spread_far(j):
        for k in range(1, n_req):
            send_if(
                at_edge, ag2.at[j, 0, 0, z], ag2.at[j, 0, k, z], ss_ag2r.at[j, far, k],
                rs_ag2r.at[j, far, k], {"req": r_peer(k), **z_peer(far)})

    def cross(j, k):
        c_copies[j, k] = send(
            ag2.at[j, 0, k], ag2.at[j, 1, k], ss_ag2c.at[j, k], rs_ag2c.at[j, k], {"mlp": sib})

    def unpack(j, core, k):
        base = (core * n_req + k) * span
        for level in range(n_z):
            xf[j, base + level * tp:base + (level + 1) * tp, :] = (
                ag2[j, core, k, level].astype(xf.dtype))

    for j in range(pieces):
        ag2[j, 0, 0, z] = ffn_in[:, lanes_of(j)]
        for k in range(1, n_z):
            z_copies[j, k] = send(
                ag2.at[j, 0, 0, z], ag2.at[j, 0, 0, z], ss_ag2z.at[j, k], rs_ag2z.at[j, k],
                z_peer(k))
        spread_far(j)
        spread(j, 0)
    for j in range(pieces):
        for step in range(1, n_z):
            z_copies[j, step].wait_recv()
            spread(j, step)
        cross(j, 0)

    def collect(j):
        for k in range(1, n_req):
            for step in range(n_z):
                r_copies[j, step, k].wait_recv()
            cross(j, k)
            unpack(j, 0, k)

    for j in range(pieces):
        unpack(j, 0, 0)
    collect(0)
    for j in range(pieces):
        for k in range(n_req):
            c_copies[j, k].wait_recv()
            unpack(j, 1, k)
        x = xf[j].astype(BF16)
        gate = jnp.dot(x, wg[lanes_of(j), :], preferred_element_type=F32)
        if j:
            gate = gate + hg[...]
        hg[...] = gate
        if j + 1 < pieces:
            collect(j + 1)
        up = jnp.dot(x, wu[lanes_of(j), :], preferred_element_type=F32)
        if j:
            up = up + hu[...]
        hu[...] = up
    gate = hg[...]
    inner = GELU_C * (gate + 0.044715 * (gate * gate * gate))
    hid[...] = (0.5 * gate * (1.0 + jnp.tanh(inner)) * hu[...]).astype(BF16)
    loads["d"].wait()

    first, second, third, finals = {}, {}, {}, []
    half = n_req * span
    straight = {}
    last = sum_pieces - 1
    for j in range(sum_pieces):
        sums = jnp.dot(hid[...], wd[:, lanes_of(j, sum_cols)], preferred_element_type=F32)
        t1[j] = sums[half:].astype(BF16)
        acc[j] = sums[:half]
        first[j] = send(t1.at[j], u1.at[j], ss_t1.at[j], rs_t1.at[j], {"mlp": sib})
    for j in range(sum_pieces):
        first[j].wait_recv()
        both = acc[j] + u1[j].astype(F32)
        if j == last:
            for k in range(n_req):
                for level in range(n_z):
                    row = k * span + level * tp
                    t4[k, level] = both[row:row + tp].astype(BF16)
            for level in range(n_z):
                t3f[j, level] = both[level * tp:(level + 1) * tp]
            for step in z_far_first + [0]:
                for k in range(n_req - 1, -1, -1):
                    if k or step:
                        straight[k, step] = send(
                            t4.at[k, z_other(step)], u4.at[k, step], ss_t4.at[k, step],
                            rs_t4.at[k, step], {"req": r_peer(n_req - k), **z_peer(step)})
            continue
        for k in range(n_req - 1, 0, -1):
            t2[j, k] = both[k * span:(k + 1) * span].astype(BF16)
            second[j, k] = send(
                t2.at[j, k], u2.at[j, k], ss_t2.at[j, k], rs_t2.at[j, k],
                {"req": r_peer(n_req - k)})
        acc[j, 0:span] = both[:span]
    for j in range(last):
        both = acc[j, 0:span]
        for k in range(1, n_req):
            second[j, k].wait_recv()
            both = both + u2[j, k].astype(F32)
        for level in range(n_z):
            t3f[j, level] = both[level * tp:(level + 1) * tp]
            t3[j, level] = both[level * tp:(level + 1) * tp].astype(BF16)
        for k in z_far_first:
            third[j, k] = send(
                t3.at[j, z_other(k)], u3.at[j, k], ss_t3.at[j, k], rs_t3.at[j, k], z_peer(k))
    settle()
    squares = jnp.zeros((tp, 1), F32)
    for j in range(sum_pieces):
        total_j = t3f[j, z]
        for (k, step), copy in straight.items() if j == last else ():
            copy.wait_recv()
            total_j = total_j + u4[k, step].astype(F32)
        for k in range(1, n_z) if j < last else ():
            third[j, k].wait_recv()
            total_j = total_j + u3[j, k].astype(F32)
        finals.append(total_j)
        squares = squares + jnp.sum(total_j * total_j, axis=-1, keepdims=True)
    scale = lax.rsqrt(squares / width + EPS)
    for j in range(sum_pieces):
        out[:, lanes_of(j, sum_cols)] = (
            residual[:, lanes_of(j, sum_cols)] + finals[j] * scale * post_ffn_gain[:, lanes_of(j, sum_cols)]).astype(BF16)


def shards(
    n_req, n_mlp,
    tokens, segments, owners, sink_keys, sink_values, window_keys, window_values,
    attn_gain, post_attn_gain, ffn_gain, post_ffn_gain,
    w_query, w_key, w_value, w_out, w_gate, w_up, w_down,
):
    tp, width = tokens.shape
    n_z = n_mlp // 2
    group = tp * n_mlp
    span = n_z * tp
    total = group * n_req
    q_cols, kv_cols, ff = w_query.shape[1], w_key.shape[1], w_gate.shape[0]
    kv_heads = kv_cols // HD
    extra = 2 * group
    head_pieces, pieces, sum_pieces = (1, 2, 2) if n_req <= 4 else (1, 1, 1)
    head_cols, cols, sum_cols = width // head_pieces, width // pieces, width // sum_pieces

    rows_type = BF16 if tp % 2 == 0 else F32

    def v(shape, dtype=BF16):
        return pltpu.VMEM(shape, dtype)

    dma = pltpu.SemaphoreType.DMA
    scratch = [
        v(tokens.shape), pltpu.SMEM(segments.shape, jnp.int32), pltpu.SMEM(owners.shape, jnp.int32),
        v(sink_keys.shape), v(sink_values.shape)]
    scratch += [v(a.shape) for a in (
        window_keys, window_values, w_query, w_key, w_value, w_out, w_gate)]
    scratch += [v((width, ff)), v((width, ff)), v((ff, width))]
    scratch += [v((1, width), F32)] * 4
    scratch += [
        dma((16 + 2 * pieces,)),
        v((total, HD), jnp.int32), v((group, extra), jnp.int32),
        v((2, n_z, tp, width)), v((group, width), rows_type),
        v((n_req, group, q_cols)), v((extra, kv_cols), F32), v((extra, kv_cols), F32),
        v((n_req, kv_heads, group, 3 * HD)), v((n_req - 1, kv_heads, group, 3 * HD)),
        v((head_pieces, 2, span, head_cols), F32), v((head_pieces, span, head_cols)),
        v((head_pieces, span, head_cols)), v((head_pieces, n_z, tp, head_cols)),
        v((head_pieces, n_z - 1, tp, head_cols)), v((head_pieces, n_z, tp, head_cols), F32),
        v((pieces, 2, n_req, n_z, tp, cols)), v((pieces, total, cols), rows_type),
        v((total, ff), F32), v((total, ff), F32), v((total, ff)),
        v((sum_pieces, n_req * span, sum_cols), F32),
        v((sum_pieces, n_req * span, sum_cols)), v((sum_pieces, n_req * span, sum_cols)),
        v((sum_pieces, n_req, span, sum_cols)), v((sum_pieces, n_req, span, sum_cols)),
        v((sum_pieces, n_z, tp, sum_cols), F32), v((sum_pieces, n_z, tp, sum_cols)), v((sum_pieces, n_z, tp, sum_cols)),
        v((n_req, n_z, tp, sum_cols)), v((n_req, n_z, tp, sum_cols)),
        dma((n_z,)), dma((n_z,)), dma((n_z,)), dma((n_z,)),
        dma((n_req,)), dma((n_req,)), dma((kv_heads, n_req)), dma((kv_heads, n_req)),
        dma((head_pieces,)), dma((head_pieces,)), dma((head_pieces, n_z)), dma((head_pieces, n_z)),
        dma((pieces, n_z)), dma((pieces, n_z)),
        dma((pieces, n_z, n_req)), dma((pieces, n_z, n_req)),
        dma((pieces, n_req)), dma((pieces, n_req)),
        dma((sum_pieces,)), dma((sum_pieces,)), dma((sum_pieces, n_req)), dma((sum_pieces, n_req)),
        dma((sum_pieces, n_z)), dma((sum_pieces, n_z)), dma((n_req, n_z)), dma((n_req, n_z)),
    ]
    hbm = pl.BlockSpec(memory_space=pl.ANY)
    return pl.pallas_call(
        functools.partial(kernel, n_req, n_mlp),
        name="layer",
        out_shape=pltpu.VMEM((tp, width), BF16),
        in_specs=[hbm] * 18,
        out_specs=pl.BlockSpec(memory_space=pltpu.VMEM),
        scratch_shapes=scratch,
        compiler_params=pltpu.CompilerParams(
            collective_id=0, has_side_effects=True, vmem_limit_bytes=62 << 20),
    )(
        tokens, segments, owners, sink_keys, sink_values,
        attn_gain, post_attn_gain, ffn_gain, post_ffn_gain,
        window_keys, window_values, w_query, w_key, w_value, w_out, w_gate, w_up, w_down,
    )


def solution(mesh):
    both = P(("req", "mlp"), None)
    return jax.shard_map(
        functools.partial(shards, mesh.shape["req"], mesh.shape["mlp"]),
        mesh=mesh,
        in_specs=(
            both, P(), P(), P(None, "mlp"), P(None, "mlp"), P("req", "mlp"), P("req", "mlp"),
            P(), P(), P(), P(),
            P(None, "mlp"), P(None, "mlp"), P(None, "mlp"), P("mlp", None), both, both, both,
        ),
        out_specs=both,
        check_vma=False,
    )
```

```python
import functools
import math

import jax
import jax.numpy as jnp
from jax import lax
from jax.experimental import pallas as pl
from jax.experimental.pallas import tpu as pltpu
from jax.sharding import PartitionSpec as P

HD = 128
EPS = 1e-06
SOFT_CAP = 50.0
SCORE_SCALE = 1.0 / (12.0 * SOFT_CAP)
MESH = pl.DeviceIdType.MESH
F32 = jnp.float32
BF16 = jnp.bfloat16
NT = (((1,), (1,)), ((), ()))
GELU_C = math.sqrt(2.0 / math.pi)


def rms_scale(values):
    return values * lax.rsqrt(jnp.mean(values * values, axis=-1, keepdims=True) + EPS)


def weights_of(scores):
    return jnp.exp(SOFT_CAP * jnp.tanh(scores * SCORE_SCALE))


def chunks(total, size):
    return [(start, min(size, total - start)) for start in range(0, total, size)]


def kernel(
    n_req, n_mlp,
    tok_hbm, seg_hbm, own_hbm, sk_hbm, sv_hbm, gains_a, gains_pa, gains_f, gains_pf,
    wk_hbm, wv_hbm, wq_hbm, wkey_hbm, wval_hbm, wo_hbm, wg_hbm, wu_hbm, wd_hbm,
    out,
    tok, segments, owners, sink_k, sink_v,
    win_k, win_v, wq, wkey, wval, wo, stage, wg, wu, wd,
    attn_gain, post_attn_gain, ffn_gain, post_ffn_gain, load_sem,
    posv, segv,
    ag1, xr, qbuf, ekf, evf, psend, prec,
    pj, s1, r1, s3, r3, head_sum,
    ag2, xf, hg, hu, hid, acc,
    t1, u1, t2, u2, t3f, t3, u3, t4, u4,
    ss_ag1z, rs_ag1z, ss_ag1c, rs_ag1c, ss_q, rs_q, ss_p, rs_p,
    ss_1, rs_1, ss_3, rs_3,
    ss_ag2z, rs_ag2z, ss_ag2r, rs_ag2r, ss_ag2c, rs_ag2c,
    ss_t1, rs_t1, ss_t2, rs_t2, ss_t3, rs_t3, ss_t4, rs_t4,
):
    n_z = n_mlp // 2
    rq = lax.axis_index("req")
    me = lax.axis_index("mlp")
    z = me // 2
    c = me % 2
    oc = 1 - c
    sib = z * 2 + oc
    tp, width = tok.shape
    group = tp * n_mlp
    span = n_z * tp
    total = group * n_req
    kv_cols = wkey.shape[1]
    q_cols = wq.shape[1]
    kv_heads = kv_cols // HD
    pieces, cols = ag2.shape[0], ag2.shape[-1]
    head_pieces, head_cols = pj.shape[0], pj.shape[-1]
    sum_pieces, sum_cols = acc.shape[0], acc.shape[-1]

    def z_other(step):
        index, weight = 0, 1
        while weight < n_z:
            bit = (z // weight) % 2
            index = index + weight * (1 - bit if step & weight else bit)
            weight *= 2
        return index

    def z_peer(step):
        return {"mlp": z_other(step) * 2 + c}

    def r_peer(step):
        return lax.rem(rq + step, n_req)

    z_far_first = list(range(n_z - 1, 0, -1))
    far = n_z - 1
    at_edge = (z == 0) | (z == far)

    barrier = pltpu.get_barrier_semaphore()
    for step in z_far_first:
        pl.semaphore_signal(barrier, inc=1, device_id=z_peer(step), device_id_type=MESH)
    for step in range(1, n_req):
        pl.semaphore_signal(barrier, inc=1, device_id={"req": r_peer(step)}, device_id_type=MESH)
    pl.semaphore_signal(barrier, inc=1, device_id={"mlp": sib}, device_id_type=MESH)

    def lanes_of(j, size=cols):
        return slice(j * size, (j + 1) * size)

    gate_loads = [
        (("g", j), wg_hbm.at[:, lanes_of(j)], stage.at[:, lanes_of(j)]) for j in range(pieces)]
    up_loads = [(("u", j), wu_hbm.at[:, lanes_of(j)], wd.at[:, lanes_of(j)]) for j in range(pieces)]
    turn_cols = math.gcd(384, cols)
    to_turn = [
        (name, raw, turned, start)
        for name, raw, turned in (("g", stage, wg), ("u", wd, wu))
        for start in range(0, width, turn_cols)]
    n_turns = len(to_turn)

    def turn(share):
        for _ in range(min(len(to_turn), max(1, n_turns * share // 24)) if share else len(to_turn)):
            name, raw, turned, start = to_turn.pop(0)
            if start % cols == 0:
                loads[name, start // cols].wait()
            turned[start:start + turn_cols, :] = raw[:, start:start + turn_cols].T

    loads = {}
    for number, (name, src, dst) in enumerate((
        ("tok", tok_hbm, tok), ("ga", gains_a, attn_gain.at[0]),
        ("seg", seg_hbm, segments), ("own", own_hbm, owners),
        *gate_loads[:2],
        ("q", wq_hbm, wq), ("k", wkey_hbm, wkey), ("v", wval_hbm, wval),
        ("sk", sk_hbm, sink_k), ("sv", sv_hbm, sink_v),
        ("wk", wk_hbm, win_k), ("wv", wv_hbm, win_v),
        *gate_loads[2:], *up_loads, ("o", wo_hbm, wo),
        ("gpa", gains_pa, post_attn_gain.at[0]), ("gf", gains_f, ffn_gain.at[0]),
        ("gpf", gains_pf, post_ffn_gain.at[0]),
        ("d", wd_hbm, wd),
    )):
        loads[name] = pltpu.make_async_copy(src, dst, load_sem.at[number])
        if name != "d":
            loads[name].start()

    sent = []

    def send(src, dst, send_sem, recv_sem, device):
        copy = pltpu.make_async_remote_copy(
            src_ref=src, dst_ref=dst, send_sem=send_sem, recv_sem=recv_sem,
            device_id=device, device_id_type=MESH,
        )
        copy.start()
        sent.append(copy)
        return copy

    def send_if(wanted, *where):
        copy = pltpu.make_async_remote_copy(
            src_ref=where[0], dst_ref=where[1], send_sem=where[2], recv_sem=where[3],
            device_id=where[4], device_id_type=MESH)

        @pl.when(wanted)
        def _():
            copy.start()
        return copy

    def settle():
        for copy in sent:
            copy.wait_send()
        sent.clear()

    loads["tok"].wait()
    loads["ga"].wait()
    token_float = tok[...].astype(F32)
    ag1[c, z] = (rms_scale(token_float) * attn_gain[...]).astype(BF16)
    pl.semaphore_wait(barrier, n_z + n_req - 1)
    z_copies = {
        k: send(ag1.at[c, z], ag1.at[c, z], ss_ag1z.at[k], rs_ag1z.at[k], z_peer(k))
        for k in z_far_first
    }
    c_copies = [send(ag1.at[c, z], ag1.at[c, z], ss_ag1c.at[0], rs_ag1c.at[0], {"mlp": sib})]

    def row_of_token(t):
        device, inner = t // tp, t % tp
        return (device % 2) * span + (device // 2) * tp + inner

    loads["seg"].wait()
    loads["own"].wait()
    for g in range(n_req):
        at = jnp.int32(0)
        for t in range(group):
            if t:
                at = jnp.where(segments[g, t] == segments[g, t - 1], at + 1, 0)
            row = g * group + row_of_token(t)
            posv[row:row + 1, :] = jnp.full((1, HD), at, jnp.int32)
    extra = 2 * group
    column = lax.broadcasted_iota(jnp.int32, (group, extra), 1)
    row_at = lax.broadcasted_iota(jnp.int32, (group, extra), 0)
    seg_row = jnp.full((group, extra), -1, jnp.int32)
    column_token = jnp.full((group, extra), group, jnp.int32)
    row_token = jnp.zeros((group, extra), jnp.int32)
    for t in range(group):
        row = row_of_token(t)
        segv[row:row + 1, :] = jnp.full((1, extra), segments[rq, t], jnp.int32)
        seg_row = jnp.where(column == row, segments[rq, t], seg_row)
        column_token = jnp.where(column == row, t, column_token)
        row_token = jnp.where(row_at == row, t, row_token)
    n_sink = sink_k.shape[0]
    local = (segv[...] == seg_row) & (column_token <= row_token)
    sinks = (column >= group) & (column < group + n_sink)
    one = jnp.where(local | sinks, 1, 0)
    emask = jnp.concatenate([one, one], axis=0) > 0
    block_rows = win_k.shape[0]
    wpos = owners[rq] * block_rows + lax.broadcasted_iota(jnp.int32, (1, block_rows), 1)

    turn(4)
    for k in range(1, n_z):
        z_copies[k].wait_recv()
        block = ag1.at[c, z_other(k)]
        c_copies.append(send(block, block, ss_ag1c.at[k], rs_ag1c.at[k], {"mlp": sib}))
    for copy in c_copies:
        copy.wait_recv()
    for core in range(2):
        for level in range(n_z):
            row = core * span + level * tp
            xr[row:row + tp, :] = ag1[core, level].astype(xr.dtype)
    rows = xr[...].astype(BF16)

    loads["q"].wait()
    qbuf[rq] = jnp.dot(rows, wq[...], preferred_element_type=F32).astype(BF16)
    q_copies = [
        send(qbuf.at[rq], qbuf.at[rq], ss_q.at[k], rs_q.at[k], {"req": r_peer(k)})
        for k in range(1, n_req)
    ]
    loads["k"].wait()
    key_new = jnp.dot(rows, wkey[...], preferred_element_type=F32).astype(BF16)
    loads["v"].wait()
    value_new = jnp.dot(rows, wval[...], preferred_element_type=F32).astype(BF16)
    loads["sk"].wait()
    loads["sv"].wait()
    for target, new, sinks in ((ekf, key_new, sink_k), (evf, value_new, sink_v)):
        target[...] = jnp.zeros_like(target)
        target[0:group, :] = new.astype(F32)
        target[group:group + n_sink, :] = sinks[...].astype(F32)

    own_q = qbuf[rq]
    extra_k = ekf[...].astype(BF16)
    extra_v = evf[...].astype(BF16)
    own_num, own_den = [], []
    for j in range(kv_heads):
        lanes = slice(j * HD, (j + 1) * HD)
        pair = jnp.concatenate(
            [own_q[:, (2 * j + i) * HD:(2 * j + i + 1) * HD] for i in range(2)], axis=0)
        scores = lax.dot_general(pair, extra_k[:, lanes], NT, preferred_element_type=F32)
        weight = jnp.where(emask, weights_of(scores), 0.0)
        den = jnp.sum(weight, axis=-1, keepdims=True)
        num = jnp.dot(weight.astype(BF16), extra_v[:, lanes], preferred_element_type=F32)
        for i in range(2):
            own_num.append(num[i * group:(i + 1) * group])
            own_den.append(den[i * group:(i + 1) * group])

    visible = wpos > posv[:, 0:1]
    visible = jnp.where(visible, 1, 0)
    visible = jnp.concatenate([visible, visible], axis=0) > 0
    lane = lax.broadcasted_iota(jnp.int32, (total, HD), 1)
    loads["wk"].wait()
    loads["wv"].wait()
    turn(2)
    for copy in q_copies:
        copy.wait_recv()
    all_q = qbuf[...].reshape(total, q_cols)
    p_copies = {}
    for j in range(kv_heads):
        lanes = slice(j * HD, (j + 1) * HD)
        pair = jnp.concatenate(
            [all_q[:, (2 * j + i) * HD:(2 * j + i + 1) * HD] for i in range(2)], axis=0)
        scores = lax.dot_general(pair, win_k[:, lanes], NT, preferred_element_type=F32)
        weight = jnp.where(visible, weights_of(scores), 0.0)
        den = jnp.sum(weight, axis=-1, keepdims=True)
        num = jnp.dot(weight.astype(BF16), win_v[:, lanes], preferred_element_type=F32)
        dens = jnp.zeros((total, HD), F32)
        for i in range(2):
            rows_i = slice(i * total, (i + 1) * total)
            psend[:, j, :, i * HD:(i + 1) * HD] = num[rows_i].astype(BF16).reshape(n_req, group, HD)
            high = den[rows_i].astype(BF16).astype(F32)
            dens = jnp.where(lane == 2 * i, high, dens)
            dens = jnp.where(lane == 2 * i + 1, den[rows_i] - high, dens)
        psend[:, j, :, 2 * HD:] = dens.astype(BF16).reshape(n_req, group, HD)
        for k in range(1, n_req):
            p_copies[j, k] = send(
                psend.at[r_peer(k), j], prec.at[k - 1, j], ss_p.at[j, k], rs_p.at[j, k],
                {"req": r_peer(k)})
    turn(9)
    loads["o"].wait()
    c_copies = []
    for j in range(kv_heads):
        heads = []
        partial = psend[rq, j].astype(F32)
        for k in range(1, n_req):
            p_copies[j, k].wait_recv()
            partial = partial + prec[k - 1, j].astype(F32)
        for i in range(2):
            num = own_num[2 * j + i] + partial[:, i * HD:(i + 1) * HD]
            base = 2 * HD + 2 * i
            den = own_den[2 * j + i] + partial[:, base:base + 1] + partial[:, base + 1:base + 2]
            heads.append((num / den).astype(BF16))
        attended = jnp.concatenate(heads, axis=1)
        for i in range(head_pieces):
            product = jnp.dot(
                attended, wo[2 * j * HD:2 * (j + 1) * HD, lanes_of(i, head_cols)],
                preferred_element_type=F32).reshape(2, span, head_cols)
            pj[i] = pj[i] + product if j else product
            if j == kv_heads - 1:
                s1[i] = pj[i, oc].astype(BF16)
                c_copies.append(send(s1.at[i], r1.at[i], ss_1.at[i], rs_1.at[i], {"mlp": sib}))
    z_copies = {}
    for j in range(head_pieces):
        c_copies[j].wait_recv()
        both = pj[j, c] + r1[j].astype(F32)
        for level in range(n_z):
            head_sum[j, level] = both[level * tp:(level + 1) * tp]
            s3[j, level] = both[level * tp:(level + 1) * tp].astype(BF16)
        for k in z_far_first:
            z_copies[j, k] = send(
                s3.at[j, z_other(k)], r3.at[j, k - 1], ss_3.at[j, k], rs_3.at[j, k], z_peer(k))
    for name in ("gpa", "gf", "gpf"):
        loads[name].wait()
    turn(0)
    loads["d"].start()
    projected, residual = [], []
    squares = jnp.zeros((tp, 1), F32)
    for j in range(head_pieces):
        total_j = head_sum[j, z]
        for k in range(1, n_z):
            z_copies[j, k].wait_recv()
            total_j = total_j + r3[j, k - 1].astype(F32)
        projected.append(total_j)
        squares = squares + jnp.sum(total_j * total_j, axis=-1, keepdims=True)
    scale = lax.rsqrt(squares / width + EPS)
    squares = jnp.zeros((tp, 1), F32)
    for j in range(head_pieces):
        part = token_float[:, lanes_of(j, head_cols)] + projected[j] * scale * post_attn_gain[:, lanes_of(j, head_cols)]
        residual.append(part)
        squares = squares + jnp.sum(part * part, axis=-1, keepdims=True)
    residual = jnp.concatenate(residual, axis=1)
    ffn_in = (residual * lax.rsqrt(squares / width + EPS) * ffn_gain[...]).astype(BF16)

    z_copies, r_copies, c_copies = {}, {}, {}

    def spread(j, step):
        level = z_other(step)
        for k in range(1, n_req):
            where = (
                ag2.at[j, 0, 0, level], ag2.at[j, 0, k, level], ss_ag2r.at[j, step, k],
                rs_ag2r.at[j, step, k], {"req": r_peer(k)})
            if step == far:
                r_copies[j, step, k] = send_if(jnp.logical_not(at_edge), *where)
                sent.append(r_copies[j, step, k])
            else:
                r_copies[j, step, k] = send(*where)

    def spread_far(j):
        for k in range(1, n_req):
            send_if(
                at_edge, ag2.at[j, 0, 0, z], ag2.at[j, 0, k, z], ss_ag2r.at[j, far, k],
                rs_ag2r.at[j, far, k], {"req": r_peer(k), **z_peer(far)})

    def cross(j, k):
        c_copies[j, k] = send(
            ag2.at[j, 0, k], ag2.at[j, 1, k], ss_ag2c.at[j, k], rs_ag2c.at[j, k], {"mlp": sib})

    def unpack(j, core, k):
        base = (core * n_req + k) * span
        for level in range(n_z):
            xf[j, base + level * tp:base + (level + 1) * tp, :] = (
                ag2[j, core, k, level].astype(xf.dtype))

    for j in range(pieces):
        ag2[j, 0, 0, z] = ffn_in[:, lanes_of(j)]
        for k in range(1, n_z):
            z_copies[j, k] = send(
                ag2.at[j, 0, 0, z], ag2.at[j, 0, 0, z], ss_ag2z.at[j, k], rs_ag2z.at[j, k],
                z_peer(k))
        spread_far(j)
        spread(j, 0)
    for j in range(pieces):
        for step in range(1, n_z):
            z_copies[j, step].wait_recv()
            spread(j, step)
        cross(j, 0)

    def collect(j):
        for k in range(1, n_req):
            for step in range(n_z):
                r_copies[j, step, k].wait_recv()
            cross(j, k)
            unpack(j, 0, k)

    for j in range(pieces):
        unpack(j, 0, 0)
    collect(0)
    for j in range(pieces):
        for k in range(n_req):
            c_copies[j, k].wait_recv()
            unpack(j, 1, k)
        x = xf[j].astype(BF16)
        gate = jnp.dot(x, wg[lanes_of(j), :], preferred_element_type=F32)
        if j:
            gate = gate + hg[...]
        hg[...] = gate
        if j + 1 < pieces:
            collect(j + 1)
        up = jnp.dot(x, wu[lanes_of(j), :], preferred_element_type=F32)
        if j:
            up = up + hu[...]
        hu[...] = up
    gate = hg[...]
    inner = GELU_C * (gate + 0.044715 * (gate * gate * gate))
    hid[...] = (0.5 * gate * (1.0 + jnp.tanh(inner)) * hu[...]).astype(BF16)
    loads["d"].wait()

    first, second, third, finals = {}, {}, {}, {}
    half = n_req * span
    straight = {}
    last = sum_pieces - 1
    for j in range(sum_pieces):
        sums = jnp.dot(hid[...], wd[:, lanes_of(j, sum_cols)], preferred_element_type=F32)
        t1[j] = sums[half:].astype(BF16)
        acc[j] = sums[:half]
        first[j] = send(t1.at[j], u1.at[j], ss_t1.at[j], rs_t1.at[j], {"mlp": sib})
    for j in range(sum_pieces):
        first[j].wait_recv()
        both = acc[j] + u1[j].astype(F32)
        if j == last:
            for k in range(n_req):
                for level in range(n_z):
                    row = k * span + level * tp
                    t4[k, level] = both[row:row + tp].astype(BF16)
            for level in range(n_z):
                t3f[j, level] = both[level * tp:(level + 1) * tp]
            for step in z_far_first + [0]:
                for k in range(n_req - 1, -1, -1):
                    if k or step:
                        straight[k, step] = send(
                            t4.at[k, z_other(step)], u4.at[k, step], ss_t4.at[k, step],
                            rs_t4.at[k, step], {"req": r_peer(n_req - k), **z_peer(step)})
            continue
        for k in range(n_req - 1, 0, -1):
            t2[j, k] = both[k * span:(k + 1) * span].astype(BF16)
            second[j, k] = send(
                t2.at[j, k], u2.at[j, k], ss_t2.at[j, k], rs_t2.at[j, k],
                {"req": r_peer(n_req - k)})
        acc[j, 0:span] = both[:span]
    for j in range(last):
        both = acc[j, 0:span]
        for k in range(1, n_req):
            second[j, k].wait_recv()
            both = both + u2[j, k].astype(F32)
        for level in range(n_z):
            t3f[j, level] = both[level * tp:(level + 1) * tp]
            t3[j, level] = both[level * tp:(level + 1) * tp].astype(BF16)
        for k in z_far_first:
            third[j, k] = send(
                t3.at[j, z_other(k)], u3.at[j, k], ss_t3.at[j, k], rs_t3.at[j, k], z_peer(k))
    settle()
    squares = jnp.zeros((tp, 1), F32)
    for j in range(sum_pieces - 1, -1, -1):
        total_j = t3f[j, z]
        for (k, step), copy in reversed(straight.items()) if j == last else ():
            copy.wait_recv()
            total_j = total_j + u4[k, step].astype(F32)
        for k in range(1, n_z) if j < last else ():
            third[j, k].wait_recv()
            total_j = total_j + u3[j, k].astype(F32)
        finals[j] = total_j
        squares = squares + jnp.sum(total_j * total_j, axis=-1, keepdims=True)
    scale = lax.rsqrt(squares / width + EPS)
    for j in range(sum_pieces):
        out[:, lanes_of(j, sum_cols)] = (
            residual[:, lanes_of(j, sum_cols)] + finals[j] * scale * post_ffn_gain[:, lanes_of(j, sum_cols)]).astype(BF16)


def shards(
    n_req, n_mlp,
    tokens, segments, owners, sink_keys, sink_values, window_keys, window_values,
    attn_gain, post_attn_gain, ffn_gain, post_ffn_gain,
    w_query, w_key, w_value, w_out, w_gate, w_up, w_down,
):
    tp, width = tokens.shape
    n_z = n_mlp // 2
    group = tp * n_mlp
    span = n_z * tp
    total = group * n_req
    q_cols, kv_cols, ff = w_query.shape[1], w_key.shape[1], w_gate.shape[0]
    kv_heads = kv_cols // HD
    extra = 2 * group
    head_pieces, pieces, sum_pieces = (1, 2, 2) if n_req <= 4 else (1, 1, 1)
    head_cols, cols, sum_cols = width // head_pieces, width // pieces, width // sum_pieces

    rows_type = BF16 if tp % 2 == 0 else F32

    def v(shape, dtype=BF16):
        return pltpu.VMEM(shape, dtype)

    dma = pltpu.SemaphoreType.DMA
    scratch = [
        v(tokens.shape), pltpu.SMEM(segments.shape, jnp.int32), pltpu.SMEM(owners.shape, jnp.int32),
        v(sink_keys.shape), v(sink_values.shape)]
    scratch += [v(a.shape) for a in (
        window_keys, window_values, w_query, w_key, w_value, w_out, w_gate)]
    scratch += [v((width, ff)), v((width, ff)), v((ff, width))]
    scratch += [v((1, width), F32)] * 4
    scratch += [
        dma((16 + 2 * pieces,)),
        v((total, HD), jnp.int32), v((group, extra), jnp.int32),
        v((2, n_z, tp, width)), v((group, width), rows_type),
        v((n_req, group, q_cols)), v((extra, kv_cols), F32), v((extra, kv_cols), F32),
        v((n_req, kv_heads, group, 3 * HD)), v((n_req - 1, kv_heads, group, 3 * HD)),
        v((head_pieces, 2, span, head_cols), F32), v((head_pieces, span, head_cols)),
        v((head_pieces, span, head_cols)), v((head_pieces, n_z, tp, head_cols)),
        v((head_pieces, n_z - 1, tp, head_cols)), v((head_pieces, n_z, tp, head_cols), F32),
        v((pieces, 2, n_req, n_z, tp, cols)), v((pieces, total, cols), rows_type),
        v((total, ff), F32), v((total, ff), F32), v((total, ff)),
        v((sum_pieces, n_req * span, sum_cols), F32),
        v((sum_pieces, n_req * span, sum_cols)), v((sum_pieces, n_req * span, sum_cols)),
        v((sum_pieces, n_req, span, sum_cols)), v((sum_pieces, n_req, span, sum_cols)),
        v((sum_pieces, n_z, tp, sum_cols), F32), v((sum_pieces, n_z, tp, sum_cols)), v((sum_pieces, n_z, tp, sum_cols)),
        v((n_req, n_z, tp, sum_cols)), v((n_req, n_z, tp, sum_cols)),
        dma((n_z,)), dma((n_z,)), dma((n_z,)), dma((n_z,)),
        dma((n_req,)), dma((n_req,)), dma((kv_heads, n_req)), dma((kv_heads, n_req)),
        dma((head_pieces,)), dma((head_pieces,)), dma((head_pieces, n_z)), dma((head_pieces, n_z)),
        dma((pieces, n_z)), dma((pieces, n_z)),
        dma((pieces, n_z, n_req)), dma((pieces, n_z, n_req)),
        dma((pieces, n_req)), dma((pieces, n_req)),
        dma((sum_pieces,)), dma((sum_pieces,)), dma((sum_pieces, n_req)), dma((sum_pieces, n_req)),
        dma((sum_pieces, n_z)), dma((sum_pieces, n_z)), dma((n_req, n_z)), dma((n_req, n_z)),
    ]
    hbm = pl.BlockSpec(memory_space=pl.ANY)
    return pl.pallas_call(
        functools.partial(kernel, n_req, n_mlp),
        name="layer",
        out_shape=pltpu.VMEM((tp, width), BF16),
        in_specs=[hbm] * 18,
        out_specs=pl.BlockSpec(memory_space=pltpu.VMEM),
        scratch_shapes=scratch,
        compiler_params=pltpu.CompilerParams(
            collective_id=0, has_side_effects=True, vmem_limit_bytes=62 << 20),
    )(
        tokens, segments, owners, sink_keys, sink_values,
        attn_gain, post_attn_gain, ffn_gain, post_ffn_gain,
        window_keys, window_values, w_query, w_key, w_value, w_out, w_gate, w_up, w_down,
    )


def solution(mesh):
    both = P(("req", "mlp"), None)
    return jax.shard_map(
        functools.partial(shards, mesh.shape["req"], mesh.shape["mlp"]),
        mesh=mesh,
        in_specs=(
            both, P(), P(), P(None, "mlp"), P(None, "mlp"), P("req", "mlp"), P("req", "mlp"),
            P(), P(), P(), P(),
            P(None, "mlp"), P(None, "mlp"), P(None, "mlp"), P("mlp", None), both, both, both,
        ),
        out_specs=both,
        check_vma=False,
    )
```
